256 devices in a mesh: wire: 64 (over z, y, core), col: 4 (over x).
Axes of the slice: x: 4, y: 4, z: 8, core: 2. Of those that a mesh axis runs over, the one named last changes fastest.
Arguments:
- search: float32 [196608, 384], P('wire', 'col')
- block_values: float32 [196608, 256], P('wire'), may hold values from -0.375 to 0.375
- block_cols: int32 [3072, 4], P('wire'), may hold values from 0 to 3071, as said below
- ritz: float32 [384, 128], replicated, may hold values from -0.3125 to 0.3125
Outputs:
- new_modes: float32 [196608, 128], P('wire', 'col')
- residual: float32 [196608, 128], P('wire', 'col')
- theta: float32 [128], P('col')
- gram_stiff: float32 [384, 384], P(None, 'col')
- gram_mass: float32 [384, 384], P(None, 'col')
The draws below stay inside these ranges and needn't reach their ends.
Inputs may be any that keep to these rules, and one draw needn't show every extreme that they name: Block rows are in groups of 48, b in group g = b // 48. block_cols[b, 0] = b. Column 1 names a block row of group g. For even b, column 2 names a block row of group g + 1 and column 3 one of group g + 2; for odd b, groups g - 1 and g - 2; groups counted around the loop of all groups.
All inputs are finite; a program needn't handle non-finite values.
Results may differ from the reference program's by a relative error of at most 0.0003.
Values sent between devices are 32-bit elements; how exact they have to be, the bound alone decides.
No kernel may reach another device: no remote copies, remote signals or barrier semaphores. Data moves between devices by JAX's collectives and lax.ppermute only.
A program may use at most 64 MiB of HBM per device.

```python
import jax
import jax.numpy as jnp
from jax import lax

BLOCK = 64
SLOTS = 4
MODES = 128
BLK_DEV = 48
SEARCH = 384
NB = 3072
NROWS = 196608


def draw_search(key, part):
    first = jax.random.fold_in(key, 0)
    place = jnp.arange(NROWS, dtype=jnp.float32) / jnp.float32(NROWS)
    rising = jnp.sqrt(0.5 + place)
    base = jax.random.normal(first, (NROWS, SEARCH), jnp.float32)
    values = base * rising[:, None]
    return jnp.clip(values, -12.0, 12.0).astype(jnp.float32)


def draw_block_cols(key, part):
    key_one, key_two = jax.random.split(key, 2)
    groups = NB // BLK_DEV
    rows = jnp.arange(NB, dtype=jnp.int32)
    owner = rows // BLK_DEV
    same = owner * BLK_DEV + jax.random.randint(key_one, (NB,), 0, BLK_DEV).astype(jnp.int32)
    sign = 1 - 2 * (rows % 2)
    reach = jnp.stack([sign, 2 * sign], axis=1).astype(jnp.int32)
    target = (owner[:, None] + reach + groups) % groups
    remote = target * BLK_DEV + jax.random.randint(key_two, (NB, 2), 0, BLK_DEV).astype(jnp.int32)
    return jnp.concatenate([rows[:, None], same[:, None], remote], axis=1).astype(jnp.int32)


def block_levels(key, shape, cuts, least, high):
    def one(dim, parts):
        draws = jax.random.uniform(jax.random.fold_in(jax.random.fold_in(key, 6), dim), (parts,), jnp.float32, least / len(cuts), high / len(cuts))
        return jnp.repeat(jnp.exp(draws), shape[dim] // parts).reshape((-1,) + (1,) * (len(shape) - dim - 1))

    loudness = one(*cuts[0])
    for cut in cuts[1:]:
        loudness = loudness * one(*cut)
    return loudness


def scatter_about(key, extent, scale, most, shards=(), kind=jnp.bfloat16):
    level = block_levels(key, extent, shards, -0.22, 0.18) if shards else 1.0
    values = jax.random.normal(key, extent, jnp.float32) * scale * level
    return jnp.minimum(jnp.maximum(values, -most), most).astype(kind)


def setup_inputs(seed: int = 0) -> dict:
    keys = jax.random.split(jax.random.key(seed), 5)
    return {
        "search": draw_search(jax.random.fold_in(keys[4], 71), 0),
        "block_values": scatter_about(keys[1], (NROWS, SLOTS * BLOCK), (SLOTS * BLOCK) ** -0.5, 0.375, ((0, 64),), jnp.float32),
        "block_cols": draw_block_cols(jax.random.fold_in(keys[4], 71), 0),
        "ritz": scatter_about(keys[3], (SEARCH, MODES), SEARCH ** -0.5, 0.3125, (), jnp.float32),
    }


def reference(search, block_values, block_cols, ritz):
    high = lax.Precision.HIGHEST
    blocks = search.reshape(NB, BLOCK, SEARCH)
    groups = NB // BLK_DEV
    values = block_values.reshape(groups, BLK_DEV, BLOCK, SLOTS * BLOCK)
    columns = block_cols.reshape(groups, BLK_DEV, SLOTS)

    def one_group(pair):
        group_values, group_cols = pair
        picked = blocks[group_cols].reshape(BLK_DEV, SLOTS * BLOCK, SEARCH)
        return jnp.einsum("bik,bkc->bic", group_values, picked, precision=high)

    product = lax.map(one_group, (values, columns)).reshape(NROWS, SEARCH)
    image = 4.0 * search + product
    gram_stiff = jnp.einsum("rk,rc->kc", search, image, precision=high) / jnp.float32(NROWS)
    gram_mass = jnp.einsum("rk,rc->kc", search, search, precision=high) / jnp.float32(NROWS)
    new_modes = jnp.dot(search, ritz, precision=high, preferred_element_type=jnp.float32)
    new_image = jnp.dot(image, ritz, precision=high, preferred_element_type=jnp.float32)
    numer = jnp.sum(new_modes * new_image, axis=0)
    denom = jnp.sum(new_modes * new_modes, axis=0)
    theta = numer / denom
    residual = new_image - new_modes * theta[None, :]
    return (new_modes, residual, theta, gram_stiff, gram_mass)
```

```python
import jax
import jax.numpy as jnp
from jax import lax
from jax.sharding import Mesh, PartitionSpec as P


def shifted(array, axis, by):
    length = lax.axis_size(axis)
    return lax.ppermute(array, axis, [(i, (i + by) % length) for i in range(length)])


RING = ("y", "core")
WIRE = ("z", "y", "core")


def sum_over_wire(x):
    shape = x.shape
    flat = x.reshape(8, -1, 128)
    part = jnp.sum(lax.all_to_all(flat, RING, 0, 0, tiled=True), axis=0)
    spread = jnp.broadcast_to(part[None], (8,) + part.shape)
    part = jnp.sum(lax.all_to_all(spread, "z", 0, 0, tiled=True), axis=0)
    spread = jnp.broadcast_to(part[None], (8,) + part.shape)
    return lax.all_to_all(spread, RING, 0, 0, tiled=True).reshape(shape)


def neighbour_group(search, distance):
    return shifted(search, WIRE, distance)


def shards(search, block_values, block_cols, ritz):
    high = lax.Precision.HIGHEST
    rows, width = search.shape
    blk = block_cols.shape[0]
    block = rows // blk
    slots = block_cols.shape[1]
    col_here = lax.axis_index("col")
    wire_here = lax.axis_index(WIRE)
    wire_count = lax.axis_size(WIRE)
    extended = jnp.concatenate(
        [
            neighbour_group(search, 2),
            neighbour_group(search, 1),
            search,
            neighbour_group(search, -1),
            neighbour_group(search, -2),
        ],
        axis=0,
    )
    ext_blocks = extended.reshape(5 * blk, block, width)
    owner = block_cols // blk
    offset = (owner - wire_here + 2 + wire_count) % wire_count
    local_index = offset * blk + block_cols % blk
    picked = ext_blocks[local_index].reshape(blk, slots * block, width)
    values = block_values.reshape(blk, block, slots * block)
    product = jnp.einsum("bik,bkc->bic", values, picked, precision=high).reshape(rows, width)
    image = 4.0 * search + product
    paired = jnp.concatenate([image, search], axis=1)
    partial_gram = jnp.einsum(
        "rk,rc->kc", lax.all_gather(search, "col", axis=1, tiled=True), paired, precision=high
    )
    mine = lax.dynamic_slice_in_dim(ritz, col_here * width, width, 0)
    modes_part = jnp.dot(search, mine, precision=high, preferred_element_type=jnp.float32)
    image_part = jnp.dot(image, mine, precision=high, preferred_element_type=jnp.float32)
    new_modes, new_image = (
        lax.psum_scatter(modes_part, "col", scatter_dimension=1, tiled=True),
        lax.psum_scatter(image_part, "col", scatter_dimension=1, tiled=True),
    )
    total_rows = jnp.float32(rows * wire_count)
    gram_total = sum_over_wire(partial_gram) / total_rows
    gram_stiff = gram_total[:, :width]
    gram_mass = gram_total[:, width:]
    mine_rows = lax.dynamic_slice_in_dim(ritz, col_here * width, width, 0)
    left_stiff = jnp.einsum("ab,aj->jb", gram_stiff, ritz, precision=high)
    left_mass = jnp.einsum("ab,aj->jb", gram_mass, ritz, precision=high)
    numer_terms = jnp.sum(left_stiff * mine_rows.T, axis=1)
    denom_terms = jnp.sum(left_mass * mine_rows.T, axis=1)
    sums = lax.psum_scatter(
        jnp.stack([numer_terms, denom_terms]), "col", scatter_dimension=1, tiled=True
    )
    theta = sums[0] / sums[1]
    residual = new_image - new_modes * theta[None, :]
    return (new_modes, residual, theta, gram_stiff, gram_mass)


def solution(mesh):
    mesh = Mesh(mesh.devices.reshape(8, 4, 2, 4), WIRE + ("col",))
    placed = (P(WIRE, "col"), P(WIRE, None), P(WIRE, None), P())
    return jax.shard_map(
        shards,
        mesh=mesh,
        in_specs=placed,
        out_specs=(P(WIRE, "col"), P(WIRE, "col"), P("col"), P(None, "col"), P(None, "col")),
        check_vma=False,
    )
```

```python
import jax
import jax.numpy as jnp
from jax import lax
from jax.experimental import pallas as pl
from jax.experimental.pallas import tpu as pltpu
from jax.sharding import Mesh, PartitionSpec as P


RING = ("y", "core")
WIRE = ("z", "y", "core")
BLOCK = 64
LANES = 128
F32 = jnp.float32
NN = (((1,), (0,)), ((), ()))
NT = (((1,), (1,)), ((), ()))
VMEM = pl.BlockSpec(memory_space=pltpu.VMEM)
SMEM = pl.BlockSpec(memory_space=pltpu.SMEM)


def shifted(array, axis, by):
    length = lax.axis_size(axis)
    return lax.ppermute(array, axis, [(i, (i + by) % length) for i in range(length)])


def split(x):
    high = x.astype(jnp.bfloat16)
    return high, (x - high.astype(F32)).astype(jnp.bfloat16)


def dot3(a, b, dims):
    (ah, al), (bh, bl) = a, b
    one = lambda x, y: lax.dot_general(x, y, dims, preferred_element_type=F32)
    return one(ah, bh) + (one(ah, bl) + one(al, bh))


def low_half(shape):
    return lax.broadcasted_iota(jnp.int32, shape, 1) < BLOCK


def block_at(ref, index, half):
    tile = ref[:, pl.ds(pl.multiple_of(index // 2 * LANES, LANES), LANES)]
    return jnp.where(index % 2 == half, tile, pltpu.roll(tile, BLOCK, 1))


def pack_kernel(prev1, prev2, next1, next2, st, to_prev1, to_prev2, to_next1, to_next2):
    low = low_half((st.shape[0], LANES))

    def step(m, carry):
        for asked, slot, parity, out in (
            (prev1, 2, 0, to_prev1),
            (prev2, 3, 0, to_prev2),
            (next1, 2, 1, to_next1),
            (next2, 3, 1, to_next2),
        ):
            first = block_at(st, asked[slot, 4 * m + parity], 0)
            second = block_at(st, asked[slot, 4 * m + 2 + parity], 1)
            out[:, pl.ds(pl.multiple_of(m * LANES, LANES), LANES)] = jnp.where(low, first, second)
        return carry

    lax.fori_loop(0, to_prev1.shape[1] // LANES, step, 0)


def image_kernel(local, st, up1, up2, down1, down2, values, image):
    m = pl.program_id(0)
    width = st.shape[0]
    low = low_half((width, LANES))
    flip = lambda x: pltpu.roll(x, BLOCK, 1)
    own = [st[:, pl.ds(pl.multiple_of(m * 2 * LANES + h * LANES, LANES), LANES)] for h in range(2)]
    a, b, c, d = up1[...], up2[...], down1[...], down2[...]
    far = (
        jnp.where(low, a, flip(b)),
        jnp.where(low, c, flip(d)),
        jnp.where(low, flip(a), b),
        jnp.where(low, flip(c), d),
    )
    for h in range(2):
        left = []
        for q in (0, 1):
            mine = own[h] if q == 0 else flip(own[h])
            near = block_at(st, local[1, 4 * m + 2 * h + q], 1)
            left.append(jnp.concatenate([jnp.where(low, mine, near), far[2 * h + q]], axis=1))
        part = dot3(
            split(jnp.concatenate(left, axis=0)),
            split(values[h * LANES : (h + 1) * LANES, :]),
            NT,
        )
        image[:, h * LANES : (h + 1) * LANES] = 4.0 * own[h] + jnp.where(
            low, part[:width], part[width:]
        )


def gram_kernel(image, st, before, after, gram):
    right = split(jnp.concatenate([image[...], st[...]], axis=0))
    for i, piece in enumerate((st, before, after)):
        gram[i] = dot3(split(piece[...]), right, NT)


def late_kernel(col, gram3, opp_a, opp_b, image, st, ritz, payload, terms, gram):
    c = col[0]
    width = st.shape[0]
    right = split(jnp.concatenate([image[...], st[...]], axis=0))
    far = dot3(split(jnp.concatenate([opp_a[...], opp_b[...]], axis=0)), right, NT)
    for piece, by in ((gram3[0], 0), (gram3[1], 3), (gram3[2], 1), (far, 2)):
        start = pl.multiple_of((c + by) % 4 * width, 8)
        gram[pl.ds(start, width), :] = piece
    whole = gram[...]
    mine = ritz[pl.ds(pl.multiple_of(c * width, 8), width), :]
    nothing = jnp.zeros_like(mine)
    both = jnp.concatenate(
        [jnp.concatenate([mine, nothing], axis=1), jnp.concatenate([nothing, mine], axis=1)], axis=0
    )
    left = dot3(split(whole), split(both), NN)
    full = ritz[...]
    sums = jnp.sum(left * jnp.concatenate([full, full], axis=1), axis=0, keepdims=True)
    terms[...] = jnp.zeros_like(terms)
    terms[0:1, :] = sums[:, :LANES]
    terms[1:2, :] = sums[:, LANES:]
    turned = whole.T
    for k in range(8):
        for i in range(3):
            for j in range(3):
                payload[k, 8 * (3 * i + j) : 8 * (3 * i + j + 1), :] = turned[
                    24 * k + 8 * i : 24 * k + 8 * i + 8, j * LANES : (j + 1) * LANES
                ]


def modes_kernel(own, before, after, coef, modes):
    modes[...] = (
        dot3(split(coef[0]), split(own[...]), NN)
        + dot3(split(coef[1]), split(before[...]), NN)
        + dot3(split(coef[2]), split(after[...]), NN)
    )


def modes_late_kernel(partial, opp_a, opp_b, coef, modes):
    opp = jnp.concatenate([opp_a[...], opp_b[...]], axis=0)
    modes[...] = partial[...] + dot3(split(coef[3]), split(opp), NN)


def image_part_kernel(image, coef, own, after, opp, before):
    right = split(image[...])
    for i, out in enumerate((own, after, opp, before)):
        out[...] = dot3(split(coef[i]), right, NN)


def final_kernel(col, parts, modes, own, from_prev, from_next, stiff, mass, theta, residual):
    total = jnp.float32(196608.0)
    terms = parts[0, 72:80, :]
    for k in range(1, 8):
        terms = terms + parts[k, 72:80, :]
    quotient = terms[0:1, :] / terms[1:2, :]
    shape = (modes.shape[0], LANES)
    here = lax.broadcasted_iota(jnp.int32, shape, 1) == (
        lax.broadcasted_iota(jnp.int32, shape, 0) + col[0] * shape[0]
    )
    column = jnp.sum(jnp.where(here, jnp.broadcast_to(quotient, shape), 0.0), axis=1, keepdims=True)
    theta[...] = column
    residual[...] = own[...] + from_prev[...] + from_next[...] - column * modes[...]
    for k in range(8):
        out = stiff if k < 4 else mass
        for i in range(3):
            for j in range(3):
                at = 24 * (k % 4) + 8 * i
                out[at : at + 8, j * LANES : (j + 1) * LANES] = (
                    parts[k, 8 * (3 * i + j) : 8 * (3 * i + j + 1), :] / total
                )


def call(kernel, shapes, in_specs, **kwargs):
    many = isinstance(shapes, list)
    out = [jax.ShapeDtypeStruct(s, F32) for s in (shapes if many else [shapes])]
    specs = kwargs.pop("out_specs", [VMEM] * len(out))
    return pl.pallas_call(
        kernel,
        out_shape=out if many else out[0],
        in_specs=in_specs,
        out_specs=specs if many else specs[0],
        **kwargs,
    )


def shards(search, values, block_cols, ritz):
    rows, width = search.shape
    blk = block_cols.shape[0]
    modes = ritz.shape[1] // 4
    half = width // 2
    c = lax.axis_index("col")
    col = jnp.reshape(c, (1,)).astype(jnp.int32)
    st = search.T
    local = (block_cols % blk).T

    before = shifted(st, "col", 1)
    after = shifted(st, "col", -1)
    asked = [shifted(local, WIRE, by) for by in (1, 2, -1, -2)]

    packed = call(pack_kernel, [(width, rows // 2)] * 4, [SMEM] * 4 + [VMEM])(*asked, st)
    up1 = shifted(packed[0], WIRE, -1)
    up2 = shifted(packed[1], WIRE, -2)
    down1 = shifted(packed[2], WIRE, 1)
    down2 = shifted(packed[3], WIRE, 2)

    opp_a = shifted(before[:half], "col", 1)
    opp_b = shifted(after[half:], "col", -1)

    mine = lax.dynamic_slice_in_dim(ritz, c * modes, modes, 1).T
    coef = jnp.stack(
        [lax.dynamic_slice_in_dim(mine, (c + by) % 4 * width, width, 1) for by in (0, 3, 1, 2)]
    )
    ours = lax.dynamic_slice_in_dim(ritz, c * width, width, 0).T
    send = jnp.stack(
        [lax.dynamic_slice_in_dim(ours, (c + by) % 4 * modes, modes, 0) for by in range(4)]
    )

    tile = lambda n: pl.BlockSpec((width, n), lambda m: (0, m))
    image = call(
        image_kernel,
        (width, rows),
        [
            SMEM,
            pl.BlockSpec((width, rows), lambda m: (0, 0)),
            tile(LANES),
            tile(LANES),
            tile(LANES),
            tile(LANES),
            pl.BlockSpec((2 * LANES, values.shape[1]), lambda m: (m, 0)),
        ],
        out_specs=[tile(2 * LANES)],
        grid=(rows // (2 * LANES),),
    )(local, st, up1, up2, down1, down2, values)

    modes3 = call(modes_kernel, (modes, rows), [VMEM] * 4)(st, before, after, coef)
    part_own, part_after, part_opp, part_before = call(
        image_part_kernel, [(modes, rows)] * 4, [VMEM] * 2
    )(image, send)
    gram3 = call(gram_kernel, (3, width, 2 * width), [VMEM] * 4)(image, st, before, after)

    payload, terms = call(
        late_kernel,
        [(8, 72, LANES), (8, LANES)],
        [SMEM] + [VMEM] * 6,
        scratch_shapes=[pltpu.VMEM((4 * width, 2 * width), F32)],
    )(col, gram3, opp_a, opp_b, image, st, ritz)

    part_opp, opp_a, opp_b = lax.optimization_barrier((part_opp, opp_a, opp_b))
    around = [shifted(terms, "col", by) for by in (1, 2, 3)]
    cut = rows // 2
    from_a = shifted(part_opp[:, :cut], "col", 1)
    from_b = shifted(part_opp[:, cut:], "col", -1)
    right = jnp.concatenate([part_after[:, :cut] + from_a, part_after[:, cut:]], axis=1)
    left = jnp.concatenate([part_before[:, :cut], part_before[:, cut:] + from_b], axis=1)
    from_prev = shifted(right, "col", 1)
    from_next = shifted(left, "col", -1)
    new_modes = call(modes_late_kernel, (modes, rows), [VMEM] * 4)(modes3, opp_a, opp_b, coef)

    part = jnp.sum(lax.all_to_all(payload, RING, 0, 0, tiled=True), axis=0)
    terms = terms + around[0] + around[1] + around[2]
    part = jnp.concatenate([part, terms], axis=0)
    part = jnp.sum(
        lax.all_to_all(jnp.broadcast_to(part[None], (8,) + part.shape), "z", 0, 0, tiled=True), axis=0
    )
    parts = lax.all_to_all(jnp.broadcast_to(part[None], (8,) + part.shape), RING, 0, 0, tiled=True)

    stiff, mass, theta, residual = call(
        final_kernel,
        [(width, 4 * width), (width, 4 * width), (modes, 1), (modes, rows)],
        [SMEM] + [VMEM] * 5,
    )(col, parts, new_modes, part_own, from_prev, from_next)
    return (new_modes.T, residual.T, theta[:, 0], stiff.T, mass.T)


def solution(mesh):
    mesh = Mesh(mesh.devices.reshape(8, 4, 2, 4), WIRE + ("col",))
    return jax.shard_map(
        shards,
        mesh=mesh,
        in_specs=(P(WIRE, "col"), P(WIRE, None), P(WIRE, None), P()),
        out_specs=(P(WIRE, "col"), P(WIRE, "col"), P("col"), P(None, "col"), P(None, "col")),
        check_vma=False,
    )
```

```python
import jax
import jax.numpy as jnp
from jax import lax
from jax.experimental import pallas as pl
from jax.experimental.pallas import tpu as pltpu
from jax.sharding import Mesh, PartitionSpec as P


RING = ("zl", "y", "core")
WIRE = ("zh", "zl", "y", "core")
BLOCK = 64
PARTS = 16
TILES = 5
PAIRS = 4
LANES = 128
F32 = jnp.float32
NN = (((1,), (0,)), ((), ()))
NT = (((1,), (1,)), ((), ()))
VMEM = pl.BlockSpec(memory_space=pltpu.VMEM)
SMEM = pl.BlockSpec(memory_space=pltpu.SMEM)


def shifted(array, axis, by):
    length = lax.axis_size(axis)
    return lax.ppermute(array, axis, [(i, (i + by) % length) for i in range(length)])


def split(x):
    high = x.astype(jnp.bfloat16)
    return high, (x - high.astype(F32)).astype(jnp.bfloat16)


def dot3(a, b, dims):
    (ah, al), (bh, bl) = a, b
    one = lambda x, y: lax.dot_general(x, y, dims, preferred_element_type=F32)
    return one(ah, bh) + (one(ah, bl) + one(al, bh))


def low_half(shape):
    return lax.broadcasted_iota(jnp.int32, shape, 1) < BLOCK


def block_at(ref, index, half):
    tile = ref[:, pl.ds(pl.multiple_of(index // 2 * LANES, LANES), LANES)]
    return jnp.where(index % 2 == half, tile, pltpu.roll(tile, BLOCK, 1))


def pack_kernel(base, prev2, next2, st, to_prev2, to_next2):
    low = low_half((st.shape[0], LANES))

    def step(m, carry):
        for asked, parity, out in ((prev2, 0, to_prev2), (next2, 1, to_next2)):
            first = block_at(st, asked[3, 4 * m + parity] - base[0], 0)
            second = block_at(st, asked[3, 4 * m + 2 + parity] - base[0], 1)
            out[:, pl.ds(pl.multiple_of(m * LANES, LANES), LANES)] = jnp.where(low, first, second)
        return carry

    lax.fori_loop(0, to_prev2.shape[1] // LANES, step, 0)


def image_kernel(base, cols, st, up1, down1, up2, down2, values, image):
    m = pl.program_id(0)
    width = st.shape[0]
    pairs = values.shape[0] // LANES
    low = low_half((width, LANES))
    flip = lambda x: pltpu.roll(x, BLOCK, 1)
    for h in range(pairs):
        tile = m * pairs + h
        row = 2 * tile
        own = st[:, pl.ds(pl.multiple_of(tile * LANES, LANES), LANES)]
        left = []
        for q, (far1, far2, at) in enumerate(((up1, up2, 1), (down1, down2, 2))):
            mine = own if q == 0 else flip(own)
            near = block_at(st, cols[1, row + q] - base[0], 1)
            first = block_at(far1, cols[2, row + q] - base[at], 0)
            second = far2[:, h // 2 * LANES : (h // 2 + 1) * LANES]
            second = flip(second) if h % 2 == 0 else second
            left.append(
                jnp.concatenate([jnp.where(low, mine, near), jnp.where(low, first, second)], axis=1)
            )
        part = dot3(
            split(jnp.concatenate(left, axis=0)),
            split(values[h * LANES : (h + 1) * LANES, :]),
            NT,
        )
        image[:, h * LANES : (h + 1) * LANES] = 4.0 * own + jnp.where(low, part[:width], part[width:])


def both_rows(ritz, c, width):
    mine = ritz[pl.ds(pl.multiple_of(c * width, 8), width), :]
    nothing = jnp.zeros_like(mine)
    return split(
        jnp.concatenate(
            [jnp.concatenate([mine, nothing], axis=1), jnp.concatenate([nothing, mine], axis=1)], axis=0
        )
    )


def quotient_terms(piece, both, ritz, start):
    full = ritz[pl.ds(start, piece.shape[0]), :]
    left = dot3(split(piece), both, NN)
    return jnp.sum(left * jnp.concatenate([full, full], axis=1), axis=0, keepdims=True)


def gram_kernel(col, image, st, before, after, ritz, gram, terms):
    c = col[0]
    width = st.shape[0]
    right = split(jnp.concatenate([image[...], st[...]], axis=0))
    both = both_rows(ritz, c, width)
    total = jnp.zeros(terms.shape, F32)
    for i, (piece, by) in enumerate(((st, 0), (before, 3), (after, 1))):
        block = dot3(split(piece[...]), right, NT)
        gram[i] = block
        total = total + quotient_terms(block, both, ritz, pl.multiple_of((c + by) % 4 * width, 8))
    terms[...] = total


def late_kernel(col, gram3, terms3, opp_a, opp_b, image, st, ritz, payload, terms, gram):
    c = col[0]
    width = st.shape[0]
    right = split(jnp.concatenate([image[...], st[...]], axis=0))
    far = dot3(split(jnp.concatenate([opp_a[...], opp_b[...]], axis=0)), right, NT)
    for piece, by in ((gram3[0], 0), (gram3[1], 3), (gram3[2], 1), (far, 2)):
        gram[pl.ds(pl.multiple_of((c + by) % 4 * width, 8), width), :] = piece
    start = pl.multiple_of((c + 2) % 4 * width, 8)
    sums = terms3[...] + quotient_terms(far, both_rows(ritz, c, width), ritz, start)
    terms[...] = jnp.zeros_like(terms)
    terms[0:1, :] = sums[:, :LANES]
    terms[1:2, :] = sums[:, LANES:]
    turned = gram[...].T
    for t in range(PARTS * TILES):
        k, at = t // TILES, t % TILES * 8
        i, j = t // 3 * 8, t % 3 * LANES
        if i < turned.shape[0]:
            payload[k, at : at + 8, :] = turned[i : i + 8, j : j + LANES]
        else:
            payload[k, at : at + 8, :] = jnp.zeros((8, LANES), F32)


def modes_kernel(own, before, after, opp_a, opp_b, coef, modes):
    opp = jnp.concatenate([opp_a[...], opp_b[...]], axis=0)
    modes[...] = (
        dot3(split(coef[0]), split(own[...]), NN)
        + dot3(split(coef[1]), split(before[...]), NN)
        + dot3(split(coef[2]), split(after[...]), NN)
        + dot3(split(coef[3]), split(opp), NN)
    )


def image_part_kernel(image, coef, own, after, opp, before):
    right = split(image[...])
    for i, out in enumerate((own, after, opp, before)):
        out[...] = dot3(split(coef[i]), right, NN)


def final_kernel(col, parts, modes, own, from_prev, from_next, stiff, mass, theta, residual):
    total = jnp.float32(196608.0)
    terms = parts[0, 8 * TILES :, :]
    for k in range(1, PARTS):
        terms = terms + parts[k, 8 * TILES :, :]
    quotient = terms[0:1, :] / terms[1:2, :]
    shape = (modes.shape[0], LANES)
    here = lax.broadcasted_iota(jnp.int32, shape, 1) == (
        lax.broadcasted_iota(jnp.int32, shape, 0) + col[0] * shape[0]
    )
    column = jnp.sum(jnp.where(here, jnp.broadcast_to(quotient, shape), 0.0), axis=1, keepdims=True)
    theta[...] = column
    residual[...] = own[...] + from_prev[...] + from_next[...] - column * modes[...]
    width = stiff.shape[0]
    for t in range(2 * width // 8 * 3):
        k, at = t // TILES, t % TILES * 8
        i, j = t // 3 * 8, t % 3 * LANES
        out = stiff if i < width else mass
        out[i % width : i % width + 8, j : j + LANES] = parts[k, at : at + 8, :] / total


def call(kernel, shapes, in_specs, **kwargs):
    many = isinstance(shapes, list)
    out = [jax.ShapeDtypeStruct(s, F32) for s in (shapes if many else [shapes])]
    specs = kwargs.pop("out_specs", [VMEM] * len(out))
    return pl.pallas_call(
        kernel,
        out_shape=out if many else out[0],
        in_specs=in_specs,
        out_specs=specs if many else specs[0],
        **kwargs,
    )


def spread_out(part):
    return jnp.broadcast_to(part[None], (PARTS,) + part.shape)


def shards(search, values, block_cols, ritz):
    rows, width = search.shape
    blk = block_cols.shape[0]
    modes = ritz.shape[1] // 4
    half = width // 2
    c = lax.axis_index("col")
    w = lax.axis_index(WIRE)
    groups = lax.axis_size(WIRE)
    col = jnp.reshape(c, (1,)).astype(jnp.int32)
    base = (jnp.stack([w, (w + 1) % groups, (w + groups - 1) % groups]) * blk).astype(jnp.int32)
    st = search.T
    cols = block_cols.T

    prev2 = shifted(cols, WIRE, 2)
    next2 = shifted(cols, WIRE, -2)
    before = shifted(st, "col", 1)
    after = shifted(st, "col", -1)
    up1 = shifted(st, WIRE, -1)
    down1 = shifted(st, WIRE, 1)

    packed = call(pack_kernel, [(width, rows // 2)] * 2, [SMEM] * 3 + [VMEM])(base, prev2, next2, st)
    up2 = shifted(packed[0], WIRE, -2)
    down2 = shifted(packed[1], WIRE, 2)

    opp_a = shifted(before[:half], "col", 1)
    opp_b = shifted(after[half:], "col", -1)

    mine = lax.dynamic_slice_in_dim(ritz, c * modes, modes, 1).T
    coef = jnp.stack(
        [lax.dynamic_slice_in_dim(mine, (c + by) % 4 * width, width, 1) for by in (0, 3, 1, 2)]
    )
    ours = lax.dynamic_slice_in_dim(ritz, c * width, width, 0).T
    send = jnp.stack(
        [lax.dynamic_slice_in_dim(ours, (c + by) % 4 * modes, modes, 0) for by in range(4)]
    )

    tile = lambda n: pl.BlockSpec((width, n), lambda m: (0, m))
    whole = pl.BlockSpec((width, rows), lambda m: (0, 0))
    image = call(
        image_kernel,
        (width, rows),
        [SMEM, SMEM, whole, whole, whole]
        + [tile(PAIRS // 2 * LANES)] * 2
        + [pl.BlockSpec((PAIRS * LANES, values.shape[1]), lambda m: (m, 0))],
        out_specs=[tile(PAIRS * LANES)],
        grid=(rows // (PAIRS * LANES),),
    )(base, cols, st, up1, down1, up2, down2, values)

    gram3, terms3 = call(
        gram_kernel, [(3, width, 2 * width), (1, 2 * LANES)], [SMEM] + [VMEM] * 5
    )(col, image, st, before, after, ritz)

    payload, terms = call(
        late_kernel,
        [(PARTS, 8 * TILES, LANES), (8, LANES)],
        [SMEM] + [VMEM] * 7,
        scratch_shapes=[pltpu.VMEM((4 * width, 2 * width), F32)],
    )(col, gram3, terms3, opp_a, opp_b, image, st, ritz)

    got = lax.all_to_all(payload, RING, 0, 0, tiled=True)
    around = [shifted(terms, "col", by) for by in (1, 2, 3)]
    held, opp_a, opp_b, payload = lax.optimization_barrier((image, opp_a, opp_b, payload))
    part_own, part_after, part_opp, part_before = call(
        image_part_kernel, [(modes, rows)] * 4, [VMEM] * 2
    )(held, send)
    cut = rows // 2
    from_a = shifted(part_opp[:, :cut], "col", 1)
    from_b = shifted(part_opp[:, cut:], "col", -1)
    right = jnp.concatenate([part_after[:, :cut] + from_a, part_after[:, cut:]], axis=1)
    left = jnp.concatenate([part_before[:, :cut], part_before[:, cut:] + from_b], axis=1)
    from_prev = shifted(right, "col", 1)
    from_next = shifted(left, "col", -1)
    new_modes = call(modes_kernel, (modes, rows), [VMEM] * 6)(st, before, after, opp_a, opp_b, coef)

    part = jnp.concatenate(
        [jnp.sum(got, axis=0), terms + around[0] + around[1] + around[2]], axis=0
    )
    part = jnp.broadcast_to(part[None], (4,) + part.shape)
    part = lax.all_to_all(part, "zh", 0, 0, tiled=True)
    part = jnp.sum(part, axis=0)
    parts = lax.all_to_all(spread_out(part), RING, 0, 0, tiled=True)

    stiff, mass, theta, residual = call(
        final_kernel,
        [(width, 4 * width), (width, 4 * width), (modes, 1), (modes, rows)],
        [SMEM] + [VMEM] * 5,
    )(col, parts, new_modes, part_own, from_prev, from_next)
    return (new_modes.T, residual.T, theta[:, 0], stiff.T, mass.T)


def solution(mesh):
    mesh = Mesh(mesh.devices.reshape(4, 2, 4, 2, 4), WIRE + ("col",))
    return jax.shard_map(
        shards,
        mesh=mesh,
        in_specs=(P(WIRE, "col"), P(WIRE, None), P(WIRE, None), P()),
        out_specs=(P(WIRE, "col"), P(WIRE, "col"), P("col"), P(None, "col"), P(None, "col")),
        check_vma=False,
    )
```

```python
import jax
import jax.numpy as jnp
from jax import lax
from jax.experimental import pallas as pl
from jax.experimental.pallas import tpu as pltpu
from jax.sharding import Mesh, PartitionSpec as P


RING = ("zl", "y", "core")
WIRE = ("zh", "zl", "y", "core")
BLOCK = 64
PARTS = 16
TILES = 5
PAIRS = 4
LANES = 128
F32 = jnp.float32
NN = (((1,), (0,)), ((), ()))
NT = (((1,), (1,)), ((), ()))
VMEM = pl.BlockSpec(memory_space=pltpu.VMEM)
SMEM = pl.BlockSpec(memory_space=pltpu.SMEM)


def shifted(array, axis, by):
    length = lax.axis_size(axis)
    return lax.ppermute(array, axis, [(i, (i + by) % length) for i in range(length)])


def split(x):
    high = x.astype(jnp.bfloat16)
    return high, (x - high.astype(F32)).astype(jnp.bfloat16)


def dot3(a, b, dims):
    (ah, al), (bh, bl) = a, b
    one = lambda x, y: lax.dot_general(x, y, dims, preferred_element_type=F32)
    rows = ah.shape[0]
    first = one(jnp.concatenate([ah, al], axis=0), bh)
    return first[:rows] + (first[rows:] + one(ah, bl))


def low_half(shape):
    return lax.broadcasted_iota(jnp.int32, shape, 1) < BLOCK


def block_at(ref, index, half):
    tile = ref[:, pl.ds(pl.multiple_of(index // 2 * LANES, LANES), LANES)]
    return jnp.where(index % 2 == half, tile, pltpu.roll(tile, BLOCK, 1))


def pack_kernel(base, prev2, next2, st, to_prev2, to_next2):
    low = low_half((st.shape[0], LANES))

    def step(m, carry):
        for asked, parity, out in ((prev2, 0, to_prev2), (next2, 1, to_next2)):
            first = block_at(st, asked[3, 4 * m + parity] - base[0], 0)
            second = block_at(st, asked[3, 4 * m + 2 + parity] - base[0], 1)
            out[:, pl.ds(pl.multiple_of(m * LANES, LANES), LANES)] = jnp.where(low, first, second)
        return carry

    lax.fori_loop(0, to_prev2.shape[1] // LANES, step, 0, unroll=4)


def image_kernel(base, cols, st, up1, down1, up2, down2, values, high, low):
    m = pl.program_id(0)
    width = st.shape[0]
    pairs = values.shape[0] // LANES
    left_half = low_half((width, LANES))
    flip = lambda x: pltpu.roll(x, BLOCK, 1)
    for h in range(pairs):
        tile = m * pairs + h
        own = st[:, pl.ds(pl.multiple_of(tile * LANES, LANES), LANES)]
        left, right = [], []
        for q, (far1, far2, at) in enumerate(((up1, up2, 1), (down1, down2, 2))):
            row = 2 * tile + q
            near = block_at(st, cols[1, row] - base[0], 1 - q)
            first = jnp.where(left_half, own, near) if q == 0 else jnp.where(left_half, near, own)
            side = h % 2
            other = block_at(far1, cols[2, row] - base[at], 1 - side)
            second = far2[:, h // 2 * LANES : (h // 2 + 1) * LANES]
            second = jnp.where(left_half, second, other) if side == 0 else jnp.where(left_half, other, second)
            left.append(jnp.concatenate([first, second], axis=1))
            coef = values[(2 * h + q) * BLOCK : (2 * h + q + 1) * BLOCK, :]
            one, two = coef[:, :LANES], coef[:, LANES:]
            one = one if q == 0 else flip(one)
            two = flip(two) if side == 0 else two
            right.append(jnp.concatenate([one, two], axis=1))
        part = dot3(
            split(jnp.concatenate(left, axis=0)), split(jnp.concatenate(right, axis=0)), NT
        )
        image = 4.0 * own + jnp.where(left_half, part[:width], part[width:])
        high[:, h * LANES : (h + 1) * LANES], low[:, h * LANES : (h + 1) * LANES] = split(image)


def quotient_terms(piece, mine, ritz, start):
    left = dot3(split(piece), split(mine), NN)
    return jnp.sum(left * ritz[pl.ds(start, piece.shape[0]), :], axis=0, keepdims=True)


def piece_terms(gram, c, ritz, terms):
    width = gram.shape[1]
    at = lambda by: pl.multiple_of((c + by) % 4 * width, 8)
    mine = ritz[pl.ds(at(0), width), :]
    total = quotient_terms(gram[0], mine, ritz, at(0))
    total = total + quotient_terms(gram[1], mine, ritz, at(3))
    terms[...] = total + quotient_terms(gram[2], mine, ritz, at(1))


def mass_kernel(col, st, before, after, ritz, high, low, gram, terms):
    width = st.shape[0]
    for i, piece in enumerate((st, before, after)):
        high[i * width : (i + 1) * width, :], low[i * width : (i + 1) * width, :] = split(piece[...])
    block = dot3((high[...], low[...]), (high[:width, :], low[:width, :]), NT)
    for i in range(3):
        gram[i] = block[i * width : (i + 1) * width]
    piece_terms(gram, col[0], ritz, terms)


def stiff_kernel(col, high, low, image_high, image_low, ritz, gram, terms):
    width = image_high.shape[0]
    block = dot3((high[...], low[...]), (image_high[...], image_low[...]), NT)
    for i in range(3):
        gram[i] = block[i * width : (i + 1) * width]
    piece_terms(gram, col[0], ritz, terms)


def late_kernel(
    col, stiff3, stiff_terms, mass3, mass_terms, opp_a, opp_b, image_high, image_low, st_high, st_low,
    ritz, payload, terms, stiff, mass
):
    c = col[0]
    width = st_high.shape[0]
    far = dot3(
        split(jnp.concatenate([opp_a[...], opp_b[...]], axis=0)),
        (
            jnp.concatenate([image_high[...], st_high[...]], axis=0),
            jnp.concatenate([image_low[...], st_low[...]], axis=0),
        ),
        NT,
    )
    terms[...] = jnp.zeros_like(terms)
    at = lambda by: pl.multiple_of((c + by) % 4 * width, 8)
    mine = ritz[pl.ds(at(0), width), :]
    turned = []
    for i, (block, whole, pieces, sums) in enumerate(
        (
            (far[:, :width], stiff, stiff3, stiff_terms),
            (far[:, width:], mass, mass3, mass_terms),
        )
    ):
        for piece, by in ((pieces[0], 0), (pieces[1], 3), (pieces[2], 1), (block, 2)):
            whole[pl.ds(at(by), width), :] = piece
        terms[i : i + 1, :] = sums[...] + quotient_terms(block, mine, ritz, at(2))
        turned.append(whole[...].T)
    for t in range(PARTS * TILES):
        k, to = t // TILES, t % TILES * 8
        i, j = t // 3 * 8, t % 3 * LANES
        if i < 2 * width:
            payload[k, to : to + 8, :] = turned[i // width][i % width : i % width + 8, j : j + LANES]
        else:
            payload[k, to : to + 8, :] = jnp.zeros((8, LANES), F32)


def modes_kernel(high, low, opp_a, opp_b, coef, modes):
    rest = high.shape[0]
    opp = jnp.concatenate([opp_a[...], opp_b[...]], axis=0)
    modes[...] = dot3(split(coef[:, :rest]), (high[...], low[...]), NN) + dot3(
        split(coef[:, rest:]), split(opp), NN
    )


def image_part_kernel(high, low, coef, own, after, opp, before):
    part = dot3(split(coef[...]), (high[...], low[...]), NN)
    modes = own.shape[0]
    for i, out in enumerate((own, after, opp, before)):
        out[...] = part[i * modes : (i + 1) * modes]


def final_kernel(col, parts, modes, own, from_prev, from_next, from_opp, stiff, mass, theta, residual):
    total = jnp.float32(196608.0)
    terms = parts[0, 8 * TILES :, :]
    for k in range(1, PARTS):
        terms = terms + parts[k, 8 * TILES :, :]
    quotient = terms[0:1, :] / terms[1:2, :]
    shape = (modes.shape[0], LANES)
    here = lax.broadcasted_iota(jnp.int32, shape, 1) == (
        lax.broadcasted_iota(jnp.int32, shape, 0) + col[0] * shape[0]
    )
    column = jnp.sum(jnp.where(here, jnp.broadcast_to(quotient, shape), 0.0), axis=1, keepdims=True)
    theta[...] = pltpu.roll(
        jnp.broadcast_to(quotient, (8, LANES)), (4 - col[0]) % 4 * shape[0], 1
    )[0:1, : shape[0]]
    image = (own[...] + from_opp[...]) + (from_prev[...] + from_next[...])
    residual[...] = image - column * modes[...]
    width = stiff.shape[0]
    for t in range(2 * width // 8 * 3):
        k, at = t // TILES, t % TILES * 8
        i, j = t // 3 * 8, t % 3 * LANES
        out = stiff if i < width else mass
        out[i % width : i % width + 8, j : j + LANES] = parts[k, at : at + 8, :] / total


def call(kernel, shapes, in_specs, dtypes=None, **kwargs):
    dtypes = dtypes or [F32] * len(shapes)
    return pl.pallas_call(
        kernel,
        out_shape=[jax.ShapeDtypeStruct(s, d) for s, d in zip(shapes, dtypes)],
        in_specs=in_specs,
        out_specs=kwargs.pop("out_specs", [VMEM] * len(shapes)),
        **kwargs,
    )


def spread_out(part):
    return jnp.broadcast_to(part[None], (PARTS,) + part.shape)


def shards(search, values, block_cols, ritz):
    rows, width = search.shape
    blk = block_cols.shape[0]
    modes = ritz.shape[1] // 4
    half = width // 2
    c = lax.axis_index("col")
    w = lax.axis_index(WIRE)
    groups = lax.axis_size(WIRE)
    col = jnp.reshape(c, (1,)).astype(jnp.int32)
    base = (jnp.stack([w, (w + 1) % groups, (w + groups - 1) % groups]) * blk).astype(jnp.int32)
    st = search.T
    cols = block_cols.T

    before = shifted(st, "col", 1)
    after = shifted(st, "col", -1)
    prev2 = shifted(cols, WIRE, 2)
    next2 = shifted(cols, WIRE, -2)
    up1 = shifted(st, WIRE, -1)
    down1 = shifted(st, WIRE, 1)

    packed = call(pack_kernel, [(width, rows // 2)] * 2, [SMEM] * 3 + [VMEM])(base, prev2, next2, st)
    up2 = shifted(packed[0], WIRE, -2)
    down2 = shifted(packed[1], WIRE, 2)

    opp_a = shifted(before[:half], "col", 1)
    opp_b = shifted(after[half:], "col", -1)

    mine = lax.dynamic_slice_in_dim(ritz, c * modes, modes, 1).T
    coef = jnp.concatenate(
        [lax.dynamic_slice_in_dim(mine, (c + by) % 4 * width, width, 1) for by in (0, 3, 1, 2)], axis=1
    )
    ours = lax.dynamic_slice_in_dim(ritz, c * width, width, 0).T
    send = jnp.roll(ours, -c * modes, 0)

    high, low, mass3, mass_terms = call(
        mass_kernel,
        [(3 * width, rows), (3 * width, rows), (3, width, width), (1, LANES)],
        [SMEM] + [VMEM] * 4,
        [jnp.bfloat16, jnp.bfloat16, F32, F32],
    )(col, st, before, after, ritz)

    tile = lambda n: pl.BlockSpec((width, n), lambda m: (0, m))
    whole = pl.BlockSpec((width, rows), lambda m: (0, 0))
    image = call(
        image_kernel,
        [(width, rows)] * 2,
        [SMEM, SMEM, whole, whole, whole]
        + [tile(PAIRS // 2 * LANES)] * 2
        + [pl.BlockSpec((PAIRS * LANES, values.shape[1]), lambda m: (m, 0))],
        [jnp.bfloat16] * 2,
        out_specs=[tile(PAIRS * LANES)] * 2,
        grid=(rows // (PAIRS * LANES),),
    )(base, cols, st, up1, down1, up2, down2, values)

    stiff3, stiff_terms = call(
        stiff_kernel, [(3, width, width), (1, LANES)], [SMEM] + [VMEM] * 5
    )(col, high, low, *image, ritz)

    payload, terms = call(
        late_kernel,
        [(PARTS, 8 * TILES, LANES), (8, LANES)],
        [SMEM] + [VMEM] * 8 + [whole] * 2 + [VMEM],
        grid=(1,),
        scratch_shapes=[pltpu.VMEM((4 * width, width), F32)] * 2,
    )(col, stiff3, stiff_terms, mass3, mass_terms, opp_a, opp_b, *image, high, low, ritz)

    got = lax.all_to_all(payload, RING, 0, 0, tiled=True)
    around = [shifted(terms, "col", by) for by in (1, 2, 3)]
    image, stiff3 = lax.optimization_barrier((image, stiff3))
    part_own, part_after, part_opp, part_before = call(image_part_kernel, [(modes, rows)] * 4, [VMEM] * 3)(*image, send)
    from_prev = shifted(part_after, "col", 1)
    from_next = shifted(part_before, "col", -1)
    from_opp = shifted(part_opp, "col", 2)
    new_modes = call(modes_kernel, [(modes, rows)], [VMEM] * 5)(high, low, opp_a, opp_b, coef)[0]

    part = jnp.concatenate(
        [jnp.sum(got, axis=0), terms + around[0] + around[1] + around[2]], axis=0
    )
    part = jnp.broadcast_to(part[None], (4,) + part.shape)
    part = lax.all_to_all(part, "zh", 0, 0, tiled=True)
    part = jnp.sum(part, axis=0)
    parts = lax.all_to_all(spread_out(part), RING, 0, 0, tiled=True)

    stiff, mass, theta, residual = call(
        final_kernel,
        [(width, 4 * width), (width, 4 * width), (1, modes), (modes, rows)],
        [SMEM] + [VMEM] * 6,
    )(col, parts, new_modes, part_own, from_prev, from_next, from_opp)
    return (new_modes.T, residual.T, theta[0], stiff.T, mass.T)


def solution(mesh):
    mesh = Mesh(mesh.devices.reshape(4, 2, 4, 2, 4), WIRE + ("col",))
    return jax.shard_map(
        shards,
        mesh=mesh,
        in_specs=(P(WIRE, "col"), P(WIRE, None), P(WIRE, None), P()),
        out_specs=(P(WIRE, "col"), P(WIRE, "col"), P("col"), P(None, "col"), P(None, "col")),
        check_vma=False,
    )
```

```python
import jax
import jax.numpy as jnp
from jax import lax
from jax.experimental import pallas as pl
from jax.experimental.pallas import tpu as pltpu
from jax.sharding import Mesh, PartitionSpec as P


RING = ("zl", "y", "core")
WIRE = ("zh", "zl", "y", "core")
BLOCK = 64
PARTS = 16
TILES = 5
PAIRS = 4
LANES = 128
F32 = jnp.float32
NN = (((1,), (0,)), ((), ()))
NT = (((1,), (1,)), ((), ()))
VMEM = pl.BlockSpec(memory_space=pltpu.VMEM)
SMEM = pl.BlockSpec(memory_space=pltpu.SMEM)


def shifted(array, axis, by):
    length = lax.axis_size(axis)
    return lax.ppermute(array, axis, [(i, (i + by) % length) for i in range(length)])


def split(x):
    high = x.astype(jnp.bfloat16)
    return high, (x - high.astype(F32)).astype(jnp.bfloat16)


def dot3(a, b, dims):
    (ah, al), (bh, bl) = a, b
    one = lambda x, y: lax.dot_general(x, y, dims, preferred_element_type=F32)
    rows = ah.shape[0]
    first = one(jnp.concatenate([ah, al], axis=0), bh)
    return first[:rows] + (first[rows:] + one(ah, bl))


def lane_tile(x):
    short = LANES - x.shape[0]
    return jnp.concatenate([x, jnp.zeros((short, x.shape[1]), x.dtype)], axis=0) if short else x


def dot4(a, b):
    both = lax.dot_general(
        jnp.concatenate(a, axis=0),
        jnp.concatenate([lane_tile(b[0]), lane_tile(b[1])], axis=0),
        NT,
        preferred_element_type=F32,
    )
    rows = a[0].shape[0]
    both = both[:rows] + both[rows:]
    return both[:, :LANES] + both[:, LANES:]


def low_half(shape):
    return lax.broadcasted_iota(jnp.int32, shape, 1) < BLOCK


def block_at(ref, index, half):
    tile = ref[:, pl.ds(pl.multiple_of(index // 2 * LANES, LANES), LANES)]
    return jnp.where(index % 2 == half, tile, pltpu.roll(tile, BLOCK, 1))


def pack_kernel(base, prev2, next2, st, to_prev2, to_next2):
    low = low_half((st.shape[0], LANES))

    def step(m, carry):
        for asked, parity, out in ((prev2, 0, to_prev2), (next2, 1, to_next2)):
            first = block_at(st, asked[3, 4 * m + parity] - base[0], 0)
            second = block_at(st, asked[3, 4 * m + 2 + parity] - base[0], 1)
            out[:, pl.ds(pl.multiple_of(m * LANES, LANES), LANES)] = jnp.where(low, first, second)
        return carry

    lax.fori_loop(0, to_prev2.shape[1] // LANES, step, 0, unroll=4)


def image_kernel(
    col, base, cols, st, up1, down1, up2, down2, values, high, low, send, ritz,
    image_high, image_low, gram, terms, part_own, part_after, part_opp, part_before, sums
):
    m = pl.program_id(0)
    width = st.shape[0]
    pairs = values.shape[0] // LANES
    left_half = low_half((width, LANES))
    flip = lambda x: pltpu.roll(x, BLOCK, 1)
    images = []

    @pl.when(m == 0)
    def _():
        sums[...] = jnp.zeros_like(sums)

    for h in range(pairs):
        tile = m * pairs + h
        own = st[:, pl.ds(pl.multiple_of(tile * LANES, LANES), LANES)]
        left, right = [], []
        for q, (far1, far2, at) in enumerate(((up1, up2, 1), (down1, down2, 2))):
            row = 2 * tile + q
            near = block_at(st, cols[1, row] - base[0], 1 - q)
            first = jnp.where(left_half, own, near) if q == 0 else jnp.where(left_half, near, own)
            side = h % 2
            other = block_at(far1, cols[2, row] - base[at], 1 - side)
            second = far2[:, h // 2 * LANES : (h // 2 + 1) * LANES]
            second = jnp.where(left_half, second, other) if side == 0 else jnp.where(left_half, other, second)
            left.append(jnp.concatenate([first, second], axis=1))
            coef = values[(2 * h + q) * BLOCK : (2 * h + q + 1) * BLOCK, :]
            one, two = coef[:, :LANES], coef[:, LANES:]
            one = one if q == 0 else flip(one)
            two = flip(two) if side == 0 else two
            right.append(jnp.concatenate([one, two], axis=1))
        part = dot4(split(jnp.concatenate(left, axis=0)), split(jnp.concatenate(right, axis=0)))
        images.append(split(4.0 * own + jnp.where(left_half, part[:width], part[width:])))
        if h % 2:
            span = slice((h - 1) * LANES, (h + 1) * LANES)
            image = tuple(jnp.concatenate([images[h - 1][i], images[h][i]], axis=1) for i in range(2))
            image_high[:, span], image_low[:, span] = image
            sums[...] += dot4((high[:, span], low[:, span]), image)
            part = dot3(split(send[...]), image, NN)
            modes = part_own.shape[0]
            for i, out in enumerate((part_own, part_after, part_opp, part_before)):
                out[:, span] = part[i * modes : (i + 1) * modes]

    @pl.when(m == pl.num_programs(0) - 1)
    def _():
        for i in range(3):
            gram[i] = sums[i * width : (i + 1) * width, :width]
        piece_terms(gram, col[0], ritz, terms)


def quotient_terms(piece, mine, ritz, start):
    left = dot3(split(piece), split(mine), NN)
    return jnp.sum(left * ritz[pl.ds(start, piece.shape[0]), :], axis=0, keepdims=True)


def piece_terms(gram, c, ritz, terms):
    width = gram.shape[1]
    at = lambda by: pl.multiple_of((c + by) % 4 * width, 8)
    mine = ritz[pl.ds(at(0), width), :]
    total = quotient_terms(gram[0], mine, ritz, at(0))
    total = total + quotient_terms(gram[1], mine, ritz, at(3))
    terms[...] = total + quotient_terms(gram[2], mine, ritz, at(1))


def mass_kernel(col, st, before, after, ritz, high, low, gram, terms):
    width = st.shape[0]
    for i, piece in enumerate((st, before, after)):
        high[i * width : (i + 1) * width, :], low[i * width : (i + 1) * width, :] = split(piece[...])
    block = dot4((high[...], low[...]), (high[:width, :], low[:width, :]))
    for i in range(3):
        gram[i] = block[i * width : (i + 1) * width, :width]
    piece_terms(gram, col[0], ritz, terms)


def late_kernel(
    col, stiff3, stiff_terms, mass3, mass_terms, opp_a, opp_b, image_high, image_low, st_high, st_low,
    ritz, payload, terms, stiff, mass
):
    c = col[0]
    width = st_high.shape[0]
    far = split(jnp.concatenate([opp_a[...], opp_b[...]], axis=0))
    far_stiff = dot4(far, (image_high[...], image_low[...]))[:, :width]
    far_mass = dot4(far, (st_high[...], st_low[...]))[:, :width]
    terms[...] = jnp.zeros_like(terms)
    at = lambda by: pl.multiple_of((c + by) % 4 * width, 8)
    mine = ritz[pl.ds(at(0), width), :]
    turned = []
    for i, (block, whole, pieces, sums) in enumerate(
        (
            (far_stiff, stiff, stiff3, stiff_terms),
            (far_mass, mass, mass3, mass_terms),
        )
    ):
        for piece, by in ((pieces[0], 0), (pieces[1], 3), (pieces[2], 1), (block, 2)):
            whole[pl.ds(at(by), width), :] = piece
        terms[i : i + 1, :] = sums[...] + quotient_terms(block, mine, ritz, at(2))
        turned.append(whole[...].T)
    for t in range(PARTS * TILES):
        k, to = t // TILES, t % TILES * 8
        i, j = t // 3 * 8, t % 3 * LANES
        if i < 2 * width:
            payload[k, to : to + 8, :] = turned[i // width][i % width : i % width + 8, j : j + LANES]
        else:
            payload[k, to : to + 8, :] = jnp.zeros((8, LANES), F32)


def modes_kernel(high, low, opp_a, opp_b, coef, modes):
    rest = high.shape[0]
    opp = jnp.concatenate([opp_a[...], opp_b[...]], axis=0)
    modes[...] = dot3(split(coef[:, :rest]), (high[...], low[...]), NN) + dot3(
        split(coef[:, rest:]), split(opp), NN
    )


def final_kernel(col, parts, modes, own, from_prev, from_next, from_opp, stiff, mass, theta, residual):
    total = jnp.float32(196608.0)
    terms = parts[0, 8 * TILES :, :]
    for k in range(1, PARTS):
        terms = terms + parts[k, 8 * TILES :, :]
    quotient = terms[0:1, :] / terms[1:2, :]
    shape = (modes.shape[0], LANES)
    here = lax.broadcasted_iota(jnp.int32, shape, 1) == (
        lax.broadcasted_iota(jnp.int32, shape, 0) + col[0] * shape[0]
    )
    column = jnp.sum(jnp.where(here, jnp.broadcast_to(quotient, shape), 0.0), axis=1, keepdims=True)
    theta[...] = pltpu.roll(
        jnp.broadcast_to(quotient, (8, LANES)), (4 - col[0]) % 4 * shape[0], 1
    )[0:1, : shape[0]]
    image = (own[...] + from_opp[...]) + (from_prev[...] + from_next[...])
    residual[...] = image - column * modes[...]
    width = stiff.shape[0]
    for t in range(2 * width // 8 * 3):
        k, at = t // TILES, t % TILES * 8
        i, j = t // 3 * 8, t % 3 * LANES
        out = stiff if i < width else mass
        out[i % width : i % width + 8, j : j + LANES] = parts[k, at : at + 8, :] / total


def call(kernel, shapes, in_specs, dtypes=None, **kwargs):
    dtypes = dtypes or [F32] * len(shapes)
    return pl.pallas_call(
        kernel,
        out_shape=[jax.ShapeDtypeStruct(s, d) for s, d in zip(shapes, dtypes)],
        in_specs=in_specs,
        out_specs=kwargs.pop("out_specs", [VMEM] * len(shapes)),
        **kwargs,
    )


def spread_out(part):
    return jnp.broadcast_to(part[None], (PARTS,) + part.shape)


def shards(search, values, block_cols, ritz):
    rows, width = search.shape
    blk = block_cols.shape[0]
    modes = ritz.shape[1] // 4
    half = width // 2
    c = lax.axis_index("col")
    w = lax.axis_index(WIRE)
    groups = lax.axis_size(WIRE)
    col = jnp.reshape(c, (1,)).astype(jnp.int32)
    base = (jnp.stack([w, (w + 1) % groups, (w + groups - 1) % groups]) * blk).astype(jnp.int32)
    st = search.T
    cols = block_cols.T

    before = shifted(st, "col", 1)
    after = shifted(st, "col", -1)
    prev2 = shifted(cols, WIRE, 2)
    next2 = shifted(cols, WIRE, -2)
    up1 = shifted(st, WIRE, -1)
    down1 = shifted(st, WIRE, 1)

    packed = call(pack_kernel, [(width, rows // 2)] * 2, [SMEM] * 3 + [VMEM])(base, prev2, next2, st)
    up2 = shifted(packed[0], WIRE, -2)
    down2 = shifted(packed[1], WIRE, 2)

    opp_a = shifted(before[:half], "col", 1)
    opp_b = shifted(after[half:], "col", -1)

    mine = lax.dynamic_slice_in_dim(ritz, c * modes, modes, 1).T
    coef = jnp.concatenate(
        [lax.dynamic_slice_in_dim(mine, (c + by) % 4 * width, width, 1) for by in (0, 3, 1, 2)], axis=1
    )
    ours = lax.dynamic_slice_in_dim(ritz, c * width, width, 0).T
    send = jnp.roll(ours, -c * modes, 0)

    high, low, mass3, mass_terms = call(
        mass_kernel,
        [(3 * width, rows), (3 * width, rows), (3, width, width), (1, LANES)],
        [SMEM] + [VMEM] * 4,
        [jnp.bfloat16, jnp.bfloat16, F32, F32],
    )(col, st, before, after, ritz)

    tile = lambda n: pl.BlockSpec((width, n), lambda m: (0, m))
    whole = pl.BlockSpec((width, rows), lambda m: (0, 0))
    step_lanes = PAIRS * LANES
    *image, stiff3, stiff_terms, part_own, part_after, part_opp, part_before = call(
        image_kernel,
        [(width, rows)] * 2 + [(3, width, width), (1, LANES)] + [(modes, rows)] * 4,
        [SMEM] * 3
        + [whole] * 3
        + [tile(step_lanes // 2)] * 2
        + [pl.BlockSpec((step_lanes, values.shape[1]), lambda m: (m, 0))]
        + [pl.BlockSpec((3 * width, step_lanes), lambda m: (0, m))] * 2
        + [VMEM] * 2,
        [jnp.bfloat16] * 2 + [F32] * 6,
        out_specs=[tile(step_lanes)] * 2
        + [
            pl.BlockSpec((3, width, width), lambda m: (0, 0, 0)),
            pl.BlockSpec((1, LANES), lambda m: (0, 0)),
        ]
        + [pl.BlockSpec((modes, step_lanes), lambda m: (0, m))] * 4,
        grid=(rows // step_lanes,),
        scratch_shapes=[pltpu.VMEM((3 * width, LANES), F32)],
    )(col, base, cols, st, up1, down1, up2, down2, values, high, low, send, ritz)

    payload, terms = call(
        late_kernel,
        [(PARTS, 8 * TILES, LANES), (8, LANES)],
        [SMEM] + [VMEM] * 8 + [whole] * 2 + [VMEM],
        grid=(1,),
        scratch_shapes=[pltpu.VMEM((4 * width, width), F32)] * 2,
    )(col, stiff3, stiff_terms, mass3, mass_terms, opp_a, opp_b, *image, high, low, ritz)

    got = lax.all_to_all(payload, RING, 0, 0, tiled=True)
    around = [shifted(terms, "col", by) for by in (1, 2, 3)]
    from_prev = shifted(part_after, "col", 1)
    from_next = shifted(part_before, "col", -1)
    from_opp = shifted(part_opp, "col", 2)
    new_modes = call(modes_kernel, [(modes, rows)], [VMEM] * 5)(high, low, opp_a, opp_b, coef)[0]

    part = jnp.concatenate(
        [jnp.sum(got, axis=0), terms + around[0] + around[1] + around[2]], axis=0
    )
    part = jnp.broadcast_to(part[None], (4,) + part.shape)
    part = lax.all_to_all(part, "zh", 0, 0, tiled=True)
    part = jnp.sum(part, axis=0)
    parts = lax.all_to_all(spread_out(part), RING, 0, 0, tiled=True)

    stiff, mass, theta, residual = call(
        final_kernel,
        [(width, 4 * width), (width, 4 * width), (1, modes), (modes, rows)],
        [SMEM] + [VMEM] * 6,
    )(col, parts, new_modes, part_own, from_prev, from_next, from_opp)
    return (new_modes.T, residual.T, theta[0], stiff.T, mass.T)


def solution(mesh):
    mesh = Mesh(mesh.devices.reshape(4, 2, 4, 2, 4), WIRE + ("col",))
    return jax.shard_map(
        shards,
        mesh=mesh,
        in_specs=(P(WIRE, "col"), P(WIRE, None), P(WIRE, None), P()),
        out_specs=(P(WIRE, "col"), P(WIRE, "col"), P("col"), P(None, "col"), P(None, "col")),
        check_vma=False,
    )
```

```python
import jax
import jax.numpy as jnp
from jax import lax
from jax.experimental import pallas as pl
from jax.experimental.pallas import tpu as pltpu
from jax.sharding import Mesh, PartitionSpec as P


RING = ("zl", "y", "core")
WIRE = ("zh", "zl", "y", "core")
BLOCK = 64
PARTS = 16
TILES = 5
PAIRS = 4
LANES = 128
F32 = jnp.float32
NN = (((1,), (0,)), ((), ()))
NT = (((1,), (1,)), ((), ()))
VMEM = pl.BlockSpec(memory_space=pltpu.VMEM)
SMEM = pl.BlockSpec(memory_space=pltpu.SMEM)


def shifted(array, axis, by):
    length = lax.axis_size(axis)
    return lax.ppermute(array, axis, [(i, (i + by) % length) for i in range(length)])


def split(x):
    high = x.astype(jnp.bfloat16)
    return high, (x - high.astype(F32)).astype(jnp.bfloat16)


def dot3(a, b, dims):
    (ah, al), (bh, bl) = a, b
    one = lambda x, y: lax.dot_general(x, y, dims, preferred_element_type=F32)
    rows = ah.shape[0]
    first = one(jnp.concatenate([ah, al], axis=0), bh)
    return first[:rows] + (first[rows:] + one(ah, bl))


def lane_tile(x):
    short = LANES - x.shape[0]
    return jnp.concatenate([x, jnp.zeros((short, x.shape[1]), x.dtype)], axis=0) if short else x


def dot4(a, b):
    both = lax.dot_general(
        jnp.concatenate(a, axis=0),
        jnp.concatenate([lane_tile(b[0]), lane_tile(b[1])], axis=0),
        NT,
        preferred_element_type=F32,
    )
    rows = a[0].shape[0]
    both = both[:rows] + both[rows:]
    return both[:, :LANES] + both[:, LANES:]


def low_half(shape):
    return lax.broadcasted_iota(jnp.int32, shape, 1) < BLOCK


def block_at(ref, index, half):
    tile = ref[:, pl.ds(pl.multiple_of(index // 2 * LANES, LANES), LANES)]
    return jnp.where(index % 2 == half, tile, pltpu.roll(tile, BLOCK, 1))


def pack_kernel(base, prev2, next2, st, to_prev2, to_next2):
    low = low_half((st.shape[0], LANES))

    def step(m, carry):
        for asked, parity, out in ((prev2, 0, to_prev2), (next2, 1, to_next2)):
            first = block_at(st, asked[3, 4 * m + parity] - base[0], 0)
            second = block_at(st, asked[3, 4 * m + 2 + parity] - base[0], 1)
            out[:, pl.ds(pl.multiple_of(m * LANES, LANES), LANES)] = jnp.where(low, first, second)
        return carry

    lax.fori_loop(0, to_prev2.shape[1] // LANES, step, 0, unroll=4)


def image_kernel(
    col, base, cols, st, up1, down1, up2, down2, values, high, low, ritz,
    image_high, image_low, gram, terms, part_own, part_after, part_opp, part_before, sums, turned
):
    m = pl.program_id(0)
    width = st.shape[0]
    pairs = values.shape[0] // LANES
    left_half = low_half((width, LANES))
    flip = lambda x: pltpu.roll(x, BLOCK, 1)
    images = []

    @pl.when(m == 0)
    def _():
        sums[...] = jnp.zeros_like(sums)
        turned[...] = ritz[pl.ds(pl.multiple_of(col[0] * width, 8), width), :].T

    modes = part_own.shape[0]
    send = split(
        jnp.concatenate(
            [turned[pl.ds(pl.multiple_of((col[0] + i) % 4 * modes, 8), modes), :] for i in range(4)], axis=0
        )
    )
    for h in range(pairs):
        tile = m * pairs + h
        own = st[:, pl.ds(pl.multiple_of(tile * LANES, LANES), LANES)]
        left, right = [], []
        for q, (far1, far2, at) in enumerate(((up1, up2, 1), (down1, down2, 2))):
            row = 2 * tile + q
            near = block_at(st, cols[1, row] - base[0], 1 - q)
            first = jnp.where(left_half, own, near) if q == 0 else jnp.where(left_half, near, own)
            side = h % 2
            other = block_at(far1, cols[2, row] - base[at], 1 - side)
            second = far2[:, h // 2 * LANES : (h // 2 + 1) * LANES]
            second = jnp.where(left_half, second, other) if side == 0 else jnp.where(left_half, other, second)
            left.append(jnp.concatenate([first, second], axis=1))
            coef = values[(2 * h + q) * BLOCK : (2 * h + q + 1) * BLOCK, :]
            one, two = coef[:, :LANES], coef[:, LANES:]
            one = one if q == 0 else flip(one)
            two = flip(two) if side == 0 else two
            right.append(jnp.concatenate([one, two], axis=1))
        part = dot4(split(jnp.concatenate(left, axis=0)), split(jnp.concatenate(right, axis=0)))
        images.append(split(4.0 * own + jnp.where(left_half, part[:width], part[width:])))
        if h % 2:
            span = slice((h - 1) * LANES, (h + 1) * LANES)
            image = tuple(jnp.concatenate([images[h - 1][i], images[h][i]], axis=1) for i in range(2))
            image_high[:, span], image_low[:, span] = image
            sums[...] += dot4((high[:, span], low[:, span]), image)
            part = dot3(send, image, NN)
            for i, out in enumerate((part_own, part_after, part_opp, part_before)):
                out[:, span] = part[i * modes : (i + 1) * modes]

    @pl.when(m == pl.num_programs(0) - 1)
    def _():
        for i in range(3):
            gram[i] = sums[i * width : (i + 1) * width, :width]
        piece_terms(gram, col[0], ritz, terms)


def quotient_terms(piece, mine, ritz, start):
    left = dot3(split(piece), split(mine), NN)
    return jnp.sum(left * ritz[pl.ds(start, piece.shape[0]), :], axis=0, keepdims=True)


def piece_terms(gram, c, ritz, terms):
    width = gram.shape[1]
    at = lambda by: pl.multiple_of((c + by) % 4 * width, 8)
    mine = ritz[pl.ds(at(0), width), :]
    total = quotient_terms(gram[0], mine, ritz, at(0))
    total = total + quotient_terms(gram[1], mine, ritz, at(3))
    terms[...] = total + quotient_terms(gram[2], mine, ritz, at(1))


def mass_kernel(col, st, before_a, before_b, after_a, after_b, ritz, high, low, gram, terms):
    width = st.shape[0]
    at = 0
    for piece in (st, before_a, before_b, after_a, after_b):
        to = at + piece.shape[0]
        high[at:to, :], low[at:to, :] = split(piece[...])
        at = to
    block = dot4((high[...], low[...]), (high[:width, :], low[:width, :]))
    for i in range(3):
        gram[i] = block[i * width : (i + 1) * width, :width]
    piece_terms(gram, col[0], ritz, terms)


def late_kernel(
    col, stiff3, stiff_terms, mass3, mass_terms, opp_a, opp_b, image_high, image_low, st_high, st_low,
    ritz, payload, terms, stiff, mass
):
    c = col[0]
    width = st_high.shape[0]
    far = split(jnp.concatenate([opp_a[...], opp_b[...]], axis=0))
    far_stiff = dot4(far, (image_high[...], image_low[...]))[:, :width]
    far_mass = dot4(far, (st_high[...], st_low[...]))[:, :width]
    terms[...] = jnp.zeros_like(terms)
    at = lambda by: pl.multiple_of((c + by) % 4 * width, 8)
    mine = ritz[pl.ds(at(0), width), :]
    turned = []
    for i, (block, whole, pieces, sums) in enumerate(
        (
            (far_stiff, stiff, stiff3, stiff_terms),
            (far_mass, mass, mass3, mass_terms),
        )
    ):
        for piece, by in ((pieces[0], 0), (pieces[1], 3), (pieces[2], 1), (block, 2)):
            whole[pl.ds(at(by), width), :] = piece
        terms[i : i + 1, :] = sums[...] + quotient_terms(block, mine, ritz, at(2))
        turned.append(whole[...].T)
    for t in range(PARTS * TILES):
        k, to = t // TILES, t % TILES * 8
        i, j = t // 3 * 8, t % 3 * LANES
        if i < 2 * width:
            payload[k, to : to + 8, :] = turned[i // width][i % width : i % width + 8, j : j + LANES]
        else:
            payload[k, to : to + 8, :] = jnp.zeros((8, LANES), F32)


def modes_kernel(
    col, high, low, opp_a, opp_b, ritz, own, from_prev, from_next, from_opp, modes, image, turned
):
    rest = high.shape[0]
    width = rest // 3
    coef = []
    for by in (0, 3, 1, 2):
        turned[...] = ritz[pl.ds(pl.multiple_of((col[0] + by) % 4 * width, 8), width), :].T
        coef.append(turned[pl.ds(pl.multiple_of(col[0] * modes.shape[0], 8), modes.shape[0]), :])
    opp = jnp.concatenate([opp_a[...], opp_b[...]], axis=0)
    modes[...] = dot3(
        split(jnp.concatenate(coef[:3], axis=1)), (high[...], low[...]), NN
    ) + dot3(split(coef[3]), split(opp), NN)
    image[...] = (own[...] + from_opp[...]) + (from_prev[...] + from_next[...])


def final_kernel(col, parts, modes, image, stiff, mass, theta, residual):
    total = jnp.float32(196608.0)
    terms = parts[0, 8 * TILES :, :]
    for k in range(1, PARTS):
        terms = terms + parts[k, 8 * TILES :, :]
    quotient = terms[0:1, :] / terms[1:2, :]
    shape = (modes.shape[0], LANES)
    here = lax.broadcasted_iota(jnp.int32, shape, 1) == (
        lax.broadcasted_iota(jnp.int32, shape, 0) + col[0] * shape[0]
    )
    column = jnp.sum(jnp.where(here, jnp.broadcast_to(quotient, shape), 0.0), axis=1, keepdims=True)
    theta[...] = pltpu.roll(
        jnp.broadcast_to(quotient, (8, LANES)), (4 - col[0]) % 4 * shape[0], 1
    )[0:1, : shape[0]]
    residual[...] = image[...] - column * modes[...]
    width = stiff.shape[0]
    for t in range(2 * width // 8 * 3):
        k, at = t // TILES, t % TILES * 8
        i, j = t // 3 * 8, t % 3 * LANES
        out = stiff if i < width else mass
        out[i % width : i % width + 8, j : j + LANES] = parts[k, at : at + 8, :] / total


def call(kernel, shapes, in_specs, dtypes=None, **kwargs):
    dtypes = dtypes or [F32] * len(shapes)
    return pl.pallas_call(
        kernel,
        out_shape=[jax.ShapeDtypeStruct(s, d) for s, d in zip(shapes, dtypes)],
        in_specs=in_specs,
        out_specs=kwargs.pop("out_specs", [VMEM] * len(shapes)),
        **kwargs,
    )


def spread_out(part):
    return jnp.broadcast_to(part[None], (PARTS,) + part.shape)


def shards(search, values, block_cols, ritz):
    rows, width = search.shape
    blk = block_cols.shape[0]
    modes = ritz.shape[1] // 4
    half = width // 2
    c = lax.axis_index("col")
    w = lax.axis_index(WIRE)
    groups = lax.axis_size(WIRE)
    col = jnp.reshape(c, (1,)).astype(jnp.int32)
    base = (jnp.stack([w, (w + 1) % groups, (w + groups - 1) % groups]) * blk).astype(jnp.int32)
    st = search.T
    cols = block_cols.T

    prev2 = shifted(cols, WIRE, 2)
    next2 = shifted(cols, WIRE, -2)
    before_a = shifted(st[:half], "col", 1)
    after_b = shifted(st[half:], "col", -1)
    before_b = shifted(st[half:], "col", 1)
    after_a = shifted(st[:half], "col", -1)
    up1 = shifted(st, WIRE, -1)
    down1 = shifted(st, WIRE, 1)

    packed = call(pack_kernel, [(width, rows // 2)] * 2, [SMEM] * 3 + [VMEM])(base, prev2, next2, st)
    up2 = shifted(packed[0], WIRE, -2)
    down2 = shifted(packed[1], WIRE, 2)

    opp_a = shifted(before_a, "col", 1)
    opp_b = shifted(after_b, "col", -1)

    high, low, mass3, mass_terms = call(
        mass_kernel,
        [(3 * width, rows), (3 * width, rows), (3, width, width), (1, LANES)],
        [SMEM] + [VMEM] * 6,
        [jnp.bfloat16, jnp.bfloat16, F32, F32],
    )(col, st, before_a, before_b, after_a, after_b, ritz)

    tile = lambda n: pl.BlockSpec((width, n), lambda m: (0, m))
    whole = pl.BlockSpec((width, rows), lambda m: (0, 0))
    step_lanes = PAIRS * LANES
    *image, stiff3, stiff_terms, part_own, part_after, part_opp, part_before = call(
        image_kernel,
        [(width, rows)] * 2 + [(3, width, width), (1, LANES)] + [(modes, rows)] * 4,
        [SMEM] * 3
        + [whole] * 3
        + [tile(step_lanes // 2)] * 2
        + [pl.BlockSpec((step_lanes, values.shape[1]), lambda m: (m, 0))]
        + [pl.BlockSpec((3 * width, step_lanes), lambda m: (0, m))] * 2
        + [VMEM],
        [jnp.bfloat16] * 2 + [F32] * 6,
        out_specs=[tile(step_lanes)] * 2
        + [
            pl.BlockSpec((3, width, width), lambda m: (0, 0, 0)),
            pl.BlockSpec((1, LANES), lambda m: (0, 0)),
        ]
        + [pl.BlockSpec((modes, step_lanes), lambda m: (0, m))] * 4,
        grid=(rows // step_lanes,),
        scratch_shapes=[pltpu.VMEM((3 * width, LANES), F32), pltpu.VMEM((4 * modes, width), F32)],
    )(col, base, cols, st, up1, down1, up2, down2, values, high, low, ritz)

    payload, terms = call(
        late_kernel,
        [(PARTS, 8 * TILES, LANES), (8, LANES)],
        [SMEM] + [VMEM] * 8 + [whole] * 2 + [VMEM],
        grid=(1,),
        scratch_shapes=[pltpu.VMEM((4 * width, width), F32)] * 2,
    )(col, stiff3, stiff_terms, mass3, mass_terms, opp_a, opp_b, *image, high, low, ritz)

    got = lax.all_to_all(payload, RING, 0, 0, tiled=True)
    around = [shifted(terms, "col", by) for by in (1, 2, 3)]
    from_prev = shifted(part_after, "col", 1)
    from_next = shifted(part_before, "col", -1)
    from_opp = shifted(part_opp, "col", 2)
    new_modes, new_image = call(
        modes_kernel,
        [(modes, rows)] * 2,
        [SMEM] + [VMEM] * 9,
        scratch_shapes=[pltpu.VMEM((4 * modes, width), F32)],
    )(col, high, low, opp_a, opp_b, ritz, part_own, from_prev, from_next, from_opp)

    part = jnp.concatenate(
        [jnp.sum(got, axis=0), terms + around[0] + around[1] + around[2]], axis=0
    )
    part = jnp.broadcast_to(part[None], (4,) + part.shape)
    part = lax.all_to_all(part, "zh", 0, 0, tiled=True)
    part = jnp.sum(part, axis=0)
    parts = lax.all_to_all(spread_out(part), RING, 0, 0, tiled=True)

    stiff, mass, theta, residual = call(
        final_kernel,
        [(width, 4 * width), (width, 4 * width), (1, modes), (modes, rows)],
        [SMEM] + [VMEM] * 3,
    )(col, parts, new_modes, new_image)
    return (new_modes.T, residual.T, theta[0], stiff.T, mass.T)


def solution(mesh):
    mesh = Mesh(mesh.devices.reshape(4, 2, 4, 2, 4), WIRE + ("col",))
    return jax.shard_map(
        shards,
        mesh=mesh,
        in_specs=(P(WIRE, "col"), P(WIRE, None), P(WIRE, None), P()),
        out_specs=(P(WIRE, "col"), P(WIRE, "col"), P("col"), P(None, "col"), P(None, "col")),
        check_vma=False,
    )
```

```python
import jax
import jax.numpy as jnp
from jax import lax
from jax.experimental import pallas as pl
from jax.experimental.pallas import tpu as pltpu
from jax.sharding import Mesh, PartitionSpec as P


RING = ("zl", "y", "core")
WIRE = ("zh", "zl", "y", "core")
BLOCK = 64
PARTS = 16
TILES = 5
PAIRS = 4
LANES = 128
F32 = jnp.float32
NN = (((1,), (0,)), ((), ()))
NT = (((1,), (1,)), ((), ()))
VMEM = pl.BlockSpec(memory_space=pltpu.VMEM)
SMEM = pl.BlockSpec(memory_space=pltpu.SMEM)


def shifted(array, axis, by):
    length = lax.axis_size(axis)
    return lax.ppermute(array, axis, [(i, (i + by) % length) for i in range(length)])


def split(x):
    high = x.astype(jnp.bfloat16)
    return high, (x - high.astype(F32)).astype(jnp.bfloat16)


def dot3(a, b, dims):
    (ah, al), (bh, bl) = a, b
    one = lambda x, y: lax.dot_general(x, y, dims, preferred_element_type=F32)
    rows = ah.shape[0]
    first = one(jnp.concatenate([ah, al], axis=0), bh)
    return first[:rows] + (first[rows:] + one(ah, bl))


def lane_tile(x):
    short = LANES - x.shape[0]
    return jnp.concatenate([x, jnp.zeros((short, x.shape[1]), x.dtype)], axis=0) if short else x


def dot4(a, b):
    both = lax.dot_general(
        jnp.concatenate(a, axis=0),
        jnp.concatenate([lane_tile(b[0]), lane_tile(b[1])], axis=0),
        NT,
        preferred_element_type=F32,
    )
    rows = a[0].shape[0]
    both = both[:rows] + both[rows:]
    return both[:, :LANES] + both[:, LANES:]


def low_half(shape):
    return lax.broadcasted_iota(jnp.int32, shape, 1) < BLOCK


def block_at(ref, index, half):
    tile = ref[:, pl.ds(pl.multiple_of(index // 2 * LANES, LANES), LANES)]
    return jnp.where(index % 2 == half, tile, pltpu.roll(tile, BLOCK, 1))


def pack_kernel(base, prev2, next2, st, to_prev2, to_next2):
    low = low_half((st.shape[0], LANES))

    def step(m, carry):
        for asked, parity, out in ((prev2, 0, to_prev2), (next2, 1, to_next2)):
            first = block_at(st, asked[3, 4 * m + parity] - base[0], 0)
            second = block_at(st, asked[3, 4 * m + 2 + parity] - base[0], 1)
            out[:, pl.ds(pl.multiple_of(m * LANES, LANES), LANES)] = jnp.where(low, first, second)
        return carry

    lax.fori_loop(0, to_prev2.shape[1] // LANES, step, 0, unroll=4)


def image_kernel(
    col, base, cols, st, up1, down1, up2, down2, values, before, after, ritz,
    image_high, image_low, stiff, stiff_terms, mass, mass_terms,
    part_own, part_after, part_opp, part_before, stiff_sum, mass_sum, turned
):
    m = pl.program_id(0)
    width = st.shape[0]
    pairs = values.shape[0] // LANES
    left_half = low_half((width, LANES))
    flip = lambda x: pltpu.roll(x, BLOCK, 1)
    images, owns = [], []

    @pl.when(m == 0)
    def _():
        stiff_sum[...] = jnp.zeros_like(stiff_sum)
        mass_sum[...] = jnp.zeros_like(mass_sum)
        turned[...] = ritz[pl.ds(pl.multiple_of(col[0] * width, 8), width), :].T

    modes = part_own.shape[0]
    send = split(
        jnp.concatenate(
            [turned[pl.ds(pl.multiple_of((col[0] + i) % 4 * modes, 8), modes), :] for i in range(4)], axis=0
        )
    )
    for h in range(pairs):
        tile = m * pairs + h
        own = st[:, pl.ds(pl.multiple_of(tile * LANES, LANES), LANES)]
        owns.append(own)
        left, right = [], []
        for q, (far1, far2, at) in enumerate(((up1, up2, 1), (down1, down2, 2))):
            row = 2 * tile + q
            near = block_at(st, cols[1, row] - base[0], 1 - q)
            first = jnp.where(left_half, own, near) if q == 0 else jnp.where(left_half, near, own)
            side = h % 2
            other = block_at(far1, cols[2, row] - base[at], 1 - side)
            second = far2[:, h // 2 * LANES : (h // 2 + 1) * LANES]
            second = jnp.where(left_half, second, other) if side == 0 else jnp.where(left_half, other, second)
            left.append(jnp.concatenate([first, second], axis=1))
            coef = values[(2 * h + q) * BLOCK : (2 * h + q + 1) * BLOCK, :]
            one, two = coef[:, :LANES], coef[:, LANES:]
            one = one if q == 0 else flip(one)
            two = flip(two) if side == 0 else two
            right.append(jnp.concatenate([one, two], axis=1))
        part = dot4(split(jnp.concatenate(left, axis=0)), split(jnp.concatenate(right, axis=0)))
        images.append(split(4.0 * own + jnp.where(left_half, part[:width], part[width:])))
        if h % 2:
            span = slice((h - 1) * LANES, (h + 1) * LANES)
            image = tuple(jnp.concatenate([images[h - 1][i], images[h][i]], axis=1) for i in range(2))
            image_high[:, span], image_low[:, span] = image
            mine = jnp.concatenate(owns[h - 1 :], axis=1)
            pieces = split(jnp.concatenate([mine, before[:, span], after[:, span]], axis=0))
            mass_sum[...] += dot4(pieces, (pieces[0][:width], pieces[1][:width]))
            stiff_sum[...] += dot4(pieces, image)
            part = dot3(send, image, NN)
            for i, out in enumerate((part_own, part_after, part_opp, part_before)):
                out[:, span] = part[i * modes : (i + 1) * modes]

    @pl.when(m == pl.num_programs(0) - 1)
    def _():
        for gram, terms, total in ((stiff, stiff_terms, stiff_sum), (mass, mass_terms, mass_sum)):
            for i in range(3):
                gram[i] = total[i * width : (i + 1) * width, :width]
            piece_terms(gram, col[0], ritz, terms)


def quotient_terms(piece, mine, ritz, start):
    left = dot3(split(piece), split(mine), NN)
    return jnp.sum(left * ritz[pl.ds(start, piece.shape[0]), :], axis=0, keepdims=True)


def piece_terms(gram, c, ritz, terms):
    width = gram.shape[1]
    at = lambda by: pl.multiple_of((c + by) % 4 * width, 8)
    mine = ritz[pl.ds(at(0), width), :]
    total = quotient_terms(gram[0], mine, ritz, at(0))
    total = total + quotient_terms(gram[1], mine, ritz, at(3))
    terms[...] = total + quotient_terms(gram[2], mine, ritz, at(1))


def late_kernel(
    col, stiff3, stiff_terms, mass3, mass_terms, opp_a, opp_b, image_high, image_low, st, ritz,
    payload, terms, stiff, mass
):
    c = col[0]
    width = st.shape[0]
    far = split(jnp.concatenate([opp_a[...], opp_b[...]], axis=0))
    far_stiff = dot4(far, (image_high[...], image_low[...]))[:, :width]
    far_mass = dot4(far, split(st[...]))[:, :width]
    terms[...] = jnp.zeros_like(terms)
    at = lambda by: pl.multiple_of((c + by) % 4 * width, 8)
    mine = ritz[pl.ds(at(0), width), :]
    turned = []
    for i, (block, whole, pieces, sums) in enumerate(
        (
            (far_stiff, stiff, stiff3, stiff_terms),
            (far_mass, mass, mass3, mass_terms),
        )
    ):
        for piece, by in ((pieces[0], 0), (pieces[1], 3), (pieces[2], 1), (block, 2)):
            whole[pl.ds(at(by), width), :] = piece
        terms[i : i + 1, :] = sums[...] + quotient_terms(block, mine, ritz, at(2))
        turned.append(whole[...].T)
    for t in range(PARTS * TILES):
        k, to = t // TILES, t % TILES * 8
        i, j = t // 3 * 8, t % 3 * LANES
        if i < 2 * width:
            payload[k, to : to + 8, :] = turned[i // width][i % width : i % width + 8, j : j + LANES]
        else:
            payload[k, to : to + 8, :] = jnp.zeros((8, LANES), F32)


def modes_kernel(
    col, st, before, after, opp_a, opp_b, ritz, own, from_prev, from_next, from_opp, modes, image, turned
):
    width = st.shape[0]
    coef = []
    for by in (0, 3, 1, 2):
        turned[...] = ritz[pl.ds(pl.multiple_of((col[0] + by) % 4 * width, 8), width), :].T
        coef.append(turned[pl.ds(pl.multiple_of(col[0] * modes.shape[0], 8), modes.shape[0]), :])
    opp = jnp.concatenate([opp_a[...], opp_b[...]], axis=0)
    modes[...] = (
        dot3(split(coef[0]), split(st[...]), NN)
        + dot3(split(coef[1]), split(before[...]), NN)
        + dot3(split(coef[2]), split(after[...]), NN)
        + dot3(split(coef[3]), split(opp), NN)
    )
    image[...] = (own[...] + from_opp[...]) + (from_prev[...] + from_next[...])


def final_kernel(col, parts, modes, image, stiff, mass, theta, residual):
    total = jnp.float32(196608.0)
    terms = parts[0, 8 * TILES :, :]
    for k in range(1, PARTS):
        terms = terms + parts[k, 8 * TILES :, :]
    quotient = terms[0:1, :] / terms[1:2, :]
    shape = (modes.shape[0], LANES)
    here = lax.broadcasted_iota(jnp.int32, shape, 1) == (
        lax.broadcasted_iota(jnp.int32, shape, 0) + col[0] * shape[0]
    )
    column = jnp.sum(jnp.where(here, jnp.broadcast_to(quotient, shape), 0.0), axis=1, keepdims=True)
    theta[...] = pltpu.roll(
        jnp.broadcast_to(quotient, (8, LANES)), (4 - col[0]) % 4 * shape[0], 1
    )[0:1, : shape[0]]
    residual[...] = image[...] - column * modes[...]
    width = stiff.shape[0]
    for t in range(2 * width // 8 * 3):
        k, at = t // TILES, t % TILES * 8
        i, j = t // 3 * 8, t % 3 * LANES
        out = stiff if i < width else mass
        out[i % width : i % width + 8, j : j + LANES] = parts[k, at : at + 8, :] / total


def call(kernel, shapes, in_specs, dtypes=None, **kwargs):
    dtypes = dtypes or [F32] * len(shapes)
    return pl.pallas_call(
        kernel,
        out_shape=[jax.ShapeDtypeStruct(s, d) for s, d in zip(shapes, dtypes)],
        in_specs=in_specs,
        out_specs=kwargs.pop("out_specs", [VMEM] * len(shapes)),
        **kwargs,
    )


def spread_out(part):
    return jnp.broadcast_to(part[None], (PARTS,) + part.shape)


def shards(search, values, block_cols, ritz):
    rows, width = search.shape
    blk = block_cols.shape[0]
    modes = ritz.shape[1] // 4
    half = width // 2
    c = lax.axis_index("col")
    w = lax.axis_index(WIRE)
    groups = lax.axis_size(WIRE)
    col = jnp.reshape(c, (1,)).astype(jnp.int32)
    base = (jnp.stack([w, (w + 1) % groups, (w + groups - 1) % groups]) * blk).astype(jnp.int32)
    st = search.T
    cols = block_cols.T

    before = shifted(st, "col", 1)
    after = shifted(st, "col", -1)
    prev2 = shifted(cols, WIRE, 2)
    next2 = shifted(cols, WIRE, -2)
    up1 = shifted(st, WIRE, -1)
    down1 = shifted(st, WIRE, 1)

    packed = call(pack_kernel, [(width, rows // 2)] * 2, [SMEM] * 3 + [VMEM])(base, prev2, next2, st)
    up2 = shifted(packed[0], WIRE, -2)
    down2 = shifted(packed[1], WIRE, 2)

    opp_a = shifted(before[:half], "col", 1)
    opp_b = shifted(after[half:], "col", -1)

    tile = lambda n: pl.BlockSpec((width, n), lambda m: (0, m))
    whole = pl.BlockSpec((width, rows), lambda m: (0, 0))
    step_lanes = PAIRS * LANES
    grams = [(3, width, width), (1, LANES)] * 2
    gram_specs = [pl.BlockSpec((3, width, width), lambda m: (0, 0, 0)), pl.BlockSpec((1, LANES), lambda m: (0, 0))] * 2
    made = call(
        image_kernel,
        [(width, rows)] * 2 + grams + [(modes, rows)] * 4,
        [SMEM] * 3
        + [whole] * 3
        + [tile(step_lanes // 2)] * 2
        + [pl.BlockSpec((step_lanes, values.shape[1]), lambda m: (m, 0))]
        + [tile(step_lanes)] * 2
        + [VMEM],
        [jnp.bfloat16] * 2 + [F32] * 8,
        out_specs=[tile(step_lanes)] * 2
        + gram_specs
        + [pl.BlockSpec((modes, step_lanes), lambda m: (0, m))] * 4,
        grid=(rows // step_lanes,),
        scratch_shapes=[pltpu.VMEM((3 * width, LANES), F32)] * 2 + [pltpu.VMEM((4 * modes, width), F32)],
    )(col, base, cols, st, up1, down1, up2, down2, values, before, after, ritz)
    image, grams, (part_own, part_after, part_opp, part_before) = made[:2], made[2:6], made[6:]

    payload, terms = call(
        late_kernel,
        [(PARTS, 8 * TILES, LANES), (8, LANES)],
        [SMEM] + [VMEM] * 10,
        scratch_shapes=[pltpu.VMEM((4 * width, width), F32)] * 2,
    )(col, *grams, opp_a, opp_b, *image, st, ritz)

    got = lax.all_to_all(payload, RING, 0, 0, tiled=True)
    around = [shifted(terms, "col", by) for by in (1, 2, 3)]
    from_prev = shifted(part_after, "col", 1)
    from_next = shifted(part_before, "col", -1)
    from_opp = shifted(part_opp, "col", 2)
    new_modes, new_image = call(
        modes_kernel,
        [(modes, rows)] * 2,
        [SMEM] + [VMEM] * 10,
        scratch_shapes=[pltpu.VMEM((4 * modes, width), F32)],
    )(col, st, before, after, opp_a, opp_b, ritz, part_own, from_prev, from_next, from_opp)

    part = jnp.concatenate(
        [jnp.sum(got, axis=0), terms + around[0] + around[1] + around[2]], axis=0
    )
    part = jnp.broadcast_to(part[None], (4,) + part.shape)
    part = lax.all_to_all(part, "zh", 0, 0, tiled=True)
    part = jnp.sum(part, axis=0)
    parts = lax.all_to_all(spread_out(part), RING, 0, 0, tiled=True)

    stiff, mass, theta, residual = call(
        final_kernel,
        [(width, 4 * width), (width, 4 * width), (1, modes), (modes, rows)],
        [SMEM] + [VMEM] * 3,
    )(col, parts, new_modes, new_image)
    return (new_modes.T, residual.T, theta[0], stiff.T, mass.T)


def solution(mesh):
    mesh = Mesh(mesh.devices.reshape(4, 2, 4, 2, 4), WIRE + ("col",))
    return jax.shard_map(
        shards,
        mesh=mesh,
        in_specs=(P(WIRE, "col"), P(WIRE, None), P(WIRE, None), P()),
        out_specs=(P(WIRE, "col"), P(WIRE, "col"), P("col"), P(None, "col"), P(None, "col")),
        check_vma=False,
    )
```

```python
import functools

import jax
import jax.numpy as jnp
from jax import lax
from jax.experimental import pallas as pl
from jax.experimental.pallas import tpu as pltpu
from jax.sharding import Mesh, PartitionSpec as P


RING = ("zl", "y")
WIRE = ("zh", "zl", "y", "core")
BLOCK = 64
PARTS = 8
TILES = 5
PAIRS = 4
LANES = 128
F32 = jnp.float32
NN = (((1,), (0,)), ((), ()))
NT = (((1,), (1,)), ((), ()))
VMEM = pl.BlockSpec(memory_space=pltpu.VMEM)
SMEM = pl.BlockSpec(memory_space=pltpu.SMEM)


def shifted(array, axis, by):
    length = lax.axis_size(axis)
    return lax.ppermute(array, axis, [(i, (i + by) % length) for i in range(length)])


def split(x):
    high = x.astype(jnp.bfloat16)
    return high, (x - high.astype(F32)).astype(jnp.bfloat16)


def dot3(a, b, dims):
    (ah, al), (bh, bl) = a, b
    one = lambda x, y: lax.dot_general(x, y, dims, preferred_element_type=F32)
    rows = ah.shape[0]
    first = one(jnp.concatenate([ah, al], axis=0), bh)
    return first[:rows] + (first[rows:] + one(ah, bl))


def lane_tile(x):
    short = LANES - x.shape[0]
    return jnp.concatenate([x, jnp.zeros((short, x.shape[1]), x.dtype)], axis=0) if short else x


def dot4(a, b):
    both = lax.dot_general(
        jnp.concatenate(a, axis=0),
        jnp.concatenate([lane_tile(b[0]), lane_tile(b[1])], axis=0),
        NT,
        preferred_element_type=F32,
    )
    rows = a[0].shape[0]
    both = both[:rows] + both[rows:]
    return both[:, :LANES] + both[:, LANES:]


def low_half(shape):
    return lax.broadcasted_iota(jnp.int32, shape, 1) < BLOCK


def block_at(ref, index, half):
    tile = ref[:, pl.ds(pl.multiple_of(index // 2 * LANES, LANES), LANES)]
    return jnp.where(index % 2 == half, tile, pltpu.roll(tile, BLOCK, 1))


def group_starts(cols, count):
    blk = cols.shape[1]
    here = cols[0, 0]
    above = jnp.where(here + blk == count, 0, here + blk)
    below = jnp.where(here == 0, count - blk, here - blk)
    return here, above, below


def pack_kernel(cols, prev2, next2, st, to_prev2, to_next2):
    low = low_half((st.shape[0], LANES))
    here = cols[0, 0]

    def step(m, carry):
        for asked, parity, out in ((prev2, 0, to_prev2), (next2, 1, to_next2)):
            first = block_at(st, asked[3, 4 * m + parity] - here, 0)
            second = block_at(st, asked[3, 4 * m + 2 + parity] - here, 1)
            out[:, pl.ds(pl.multiple_of(m * LANES, LANES), LANES)] = jnp.where(low, first, second)
        return carry

    lax.fori_loop(0, to_prev2.shape[1] // LANES, step, 0, unroll=4)


def image_kernel(
    count, col, cols, st, up1, down1, up2, down2, values, before, after, ritz,
    image_high, image_low, stiff, stiff_terms, mass, mass_terms,
    part_own, part_after, part_opp, part_before, stiff_sum, mass_sum, turned
):
    m = pl.program_id(0)
    width = st.shape[0]
    pairs = values.shape[0] // LANES
    left_half = low_half((width, LANES))
    flip = lambda x: pltpu.roll(x, BLOCK, 1)
    images, owns = [], []
    base = group_starts(cols, count)

    @pl.when(m == 0)
    def _():
        stiff_sum[...] = jnp.zeros_like(stiff_sum)
        mass_sum[...] = jnp.zeros_like(mass_sum)
        turned[...] = ritz[pl.ds(pl.multiple_of(col[0] * width, 8), width), :].T

    modes = part_own.shape[0]
    send = split(
        jnp.concatenate(
            [turned[pl.ds(pl.multiple_of((col[0] + i) % 4 * modes, 8), modes), :] for i in range(4)], axis=0
        )
    )
    for h in range(pairs):
        tile = m * pairs + h
        own = st[:, pl.ds(pl.multiple_of(tile * LANES, LANES), LANES)]
        owns.append(own)
        left, right = [], []
        for q, (far1, far2, at) in enumerate(((up1, up2, 1), (down1, down2, 2))):
            row = 2 * tile + q
            near = block_at(st, cols[1, row] - base[0], 1 - q)
            first = jnp.where(left_half, own, near) if q == 0 else jnp.where(left_half, near, own)
            side = h % 2
            other = block_at(far1, cols[2, row] - base[at], 1 - side)
            second = far2[:, h // 2 * LANES : (h // 2 + 1) * LANES]
            second = jnp.where(left_half, second, other) if side == 0 else jnp.where(left_half, other, second)
            left.append(jnp.concatenate([first, second], axis=1))
            coef = values[(2 * h + q) * BLOCK : (2 * h + q + 1) * BLOCK, :]
            one, two = coef[:, :LANES], coef[:, LANES:]
            one = one if q == 0 else flip(one)
            two = flip(two) if side == 0 else two
            right.append(jnp.concatenate([one, two], axis=1))
        part = dot4(split(jnp.concatenate(left, axis=0)), split(jnp.concatenate(right, axis=0)))
        images.append(split(4.0 * own + jnp.where(left_half, part[:width], part[width:])))
        if h % 2:
            span = slice((h - 1) * LANES, (h + 1) * LANES)
            image = tuple(jnp.concatenate([images[h - 1][i], images[h][i]], axis=1) for i in range(2))
            image_high[:, span], image_low[:, span] = image
            mine = jnp.concatenate(owns[h - 1 :], axis=1)
            pieces = split(jnp.concatenate([mine, before[:, span], after[:, span]], axis=0))
            mass_sum[...] += dot4(pieces, (pieces[0][:width], pieces[1][:width]))
            stiff_sum[...] += dot4(pieces, image)
            part = dot3(send, image, NN)
            for i, out in enumerate((part_own, part_after, part_opp, part_before)):
                out[:, span] = part[i * modes : (i + 1) * modes]

    @pl.when(m == pl.num_programs(0) - 1)
    def _():
        for gram, terms, total in ((stiff, stiff_terms, stiff_sum), (mass, mass_terms, mass_sum)):
            for i in range(3):
                gram[i] = total[i * width : (i + 1) * width, :width]
            piece_terms(gram, col[0], ritz, terms)


def quotient_terms(piece, mine, ritz, start):
    left = dot3(split(piece), split(mine), NN)
    return jnp.sum(left * ritz[pl.ds(start, piece.shape[0]), :], axis=0, keepdims=True)


def piece_terms(gram, c, ritz, terms):
    width = gram.shape[1]
    at = lambda by: pl.multiple_of((c + by) % 4 * width, 8)
    mine = ritz[pl.ds(at(0), width), :]
    total = quotient_terms(gram[0], mine, ritz, at(0))
    total = total + quotient_terms(gram[1], mine, ritz, at(3))
    terms[...] = total + quotient_terms(gram[2], mine, ritz, at(1))


def late_kernel(
    place, stiff3, stiff_terms, mass3, mass_terms, opp_a, opp_b, image_high, image_low, st, ritz,
    kept, given, terms, stiff, mass
):
    c = place[0]
    width = st.shape[0]
    far = split(jnp.concatenate([opp_a[...], opp_b[...]], axis=0))
    far_stiff = dot4(far, (image_high[...], image_low[...]))[:, :width]
    far_mass = dot4(far, split(st[...]))[:, :width]
    terms[...] = jnp.zeros_like(terms)
    at = lambda by: pl.multiple_of((c + by) % 4 * width, 8)
    mine = ritz[pl.ds(at(0), width), :]
    turned = []
    for i, (block, whole, pieces, sums) in enumerate(
        (
            (far_stiff, stiff, stiff3, stiff_terms),
            (far_mass, mass, mass3, mass_terms),
        )
    ):
        for piece, by in ((pieces[0], 0), (pieces[1], 3), (pieces[2], 1), (block, 2)):
            whole[pl.ds(at(by), width), :] = piece
        terms[i : i + 1, :] = sums[...] + quotient_terms(block, mine, ritz, at(2))
        turned.append(whole[...].T)

    def gram_tile(t):
        i, j = t // 3 * 8, t % 3 * LANES
        if i >= 2 * width:
            return jnp.zeros((8, LANES), F32)
        return turned[i // width][i % width : i % width + 8, j : j + LANES]

    first = place[1] == 0
    for t in range(PARTS * TILES):
        k, to = t // TILES, t % TILES * 8
        zero, one = gram_tile(t), gram_tile(t + PARTS * TILES)
        kept[k, to : to + 8, :] = jnp.where(first, zero, one)
        given[k, to : to + 8, :] = jnp.where(first, one, zero)


def modes_kernel(
    col, st, before, after, opp_a, opp_b, ritz, own, from_prev, from_next, from_opp, modes, image, turned
):
    width = st.shape[0]
    coef = []
    for by in (0, 3, 1, 2):
        turned[...] = ritz[pl.ds(pl.multiple_of((col[0] + by) % 4 * width, 8), width), :].T
        coef.append(turned[pl.ds(pl.multiple_of(col[0] * modes.shape[0], 8), modes.shape[0]), :])
    opp = jnp.concatenate([opp_a[...], opp_b[...]], axis=0)
    modes[...] = (
        dot3(split(coef[0]), split(st[...]), NN)
        + dot3(split(coef[1]), split(before[...]), NN)
        + dot3(split(coef[2]), split(after[...]), NN)
        + dot3(split(coef[3]), split(opp), NN)
    )
    image[...] = (own[...] + from_opp[...]) + (from_prev[...] + from_next[...])


def final_kernel(place, parts, others, modes, image, stiff, mass, theta, residual):
    total = jnp.float32(196608.0)
    first = place[1] == 0

    def part_tile(k, at):
        mine, other = parts[k % PARTS, at : at + 8, :], others[k % PARTS, at : at + 8, :]
        return jnp.where(first, mine, other) if k < PARTS else jnp.where(first, other, mine)

    terms = part_tile(0, 8 * TILES)
    for k in range(1, 2 * PARTS):
        terms = terms + part_tile(k, 8 * TILES)
    quotient = terms[0:1, :] / terms[1:2, :]
    shape = (modes.shape[0], LANES)
    here = lax.broadcasted_iota(jnp.int32, shape, 1) == (
        lax.broadcasted_iota(jnp.int32, shape, 0) + place[0] * shape[0]
    )
    column = jnp.sum(jnp.where(here, jnp.broadcast_to(quotient, shape), 0.0), axis=1, keepdims=True)
    theta[...] = pltpu.roll(
        jnp.broadcast_to(quotient, (8, LANES)), (4 - place[0]) % 4 * shape[0], 1
    )[0:1, : shape[0]]
    residual[...] = image[...] - column * modes[...]
    width = stiff.shape[0]
    for t in range(2 * width // 8 * 3):
        k, at = t // TILES, t % TILES * 8
        i, j = t // 3 * 8, t % 3 * LANES
        out = stiff if i < width else mass
        out[i % width : i % width + 8, j : j + LANES] = part_tile(k, at) / total


def call(kernel, shapes, in_specs, dtypes=None, **kwargs):
    dtypes = dtypes or [F32] * len(shapes)
    return pl.pallas_call(
        kernel,
        out_shape=[jax.ShapeDtypeStruct(s, d) for s, d in zip(shapes, dtypes)],
        in_specs=in_specs,
        out_specs=kwargs.pop("out_specs", [VMEM] * len(shapes)),
        **kwargs,
    )


def spread_out(part):
    return jnp.broadcast_to(part[None], (PARTS,) + part.shape)


def shards(search, values, block_cols, ritz):
    rows, width = search.shape
    blk = block_cols.shape[0]
    modes = ritz.shape[1] // 4
    half = width // 2
    c = lax.axis_index("col")
    count = blk * lax.axis_size(WIRE)
    col = jnp.reshape(c, (1,)).astype(jnp.int32)
    place = jnp.stack([c, lax.axis_index("core")]).astype(jnp.int32)
    st = search.T
    cols = block_cols.T

    before = shifted(st, "col", 1)
    after = shifted(st, "col", -1)
    prev2 = shifted(cols, WIRE, 2)
    next2 = shifted(cols, WIRE, -2)
    up1 = shifted(st, WIRE, -1)
    down1 = shifted(st, WIRE, 1)

    packed = call(pack_kernel, [(width, rows // 2)] * 2, [SMEM] * 3 + [VMEM])(cols, prev2, next2, st)
    up2 = shifted(packed[0], WIRE, -2)
    down2 = shifted(packed[1], WIRE, 2)

    opp_a = shifted(before[:half], "col", 1)
    opp_b = shifted(after[half:], "col", -1)

    tile = lambda n: pl.BlockSpec((width, n), lambda m: (0, m))
    whole = pl.BlockSpec((width, rows), lambda m: (0, 0))
    step_lanes = PAIRS * LANES
    grams = [(3, width, width), (1, LANES)] * 2
    gram_specs = [pl.BlockSpec((3, width, width), lambda m: (0, 0, 0)), pl.BlockSpec((1, LANES), lambda m: (0, 0))] * 2
    made = call(
        functools.partial(image_kernel, count),
        [(width, rows)] * 2 + grams + [(modes, rows)] * 4,
        [SMEM] * 2
        + [whole] * 3
        + [tile(step_lanes // 2)] * 2
        + [pl.BlockSpec((step_lanes, values.shape[1]), lambda m: (m, 0))]
        + [tile(step_lanes)] * 2
        + [VMEM],
        [jnp.bfloat16] * 2 + [F32] * 8,
        out_specs=[tile(step_lanes)] * 2
        + gram_specs
        + [pl.BlockSpec((modes, step_lanes), lambda m: (0, m))] * 4,
        grid=(rows // step_lanes,),
        scratch_shapes=[pltpu.VMEM((3 * width, LANES), F32)] * 2 + [pltpu.VMEM((4 * modes, width), F32)],
    )(col, cols, st, up1, down1, up2, down2, values, before, after, ritz)
    image, grams, (part_own, part_after, part_opp, part_before) = made[:2], made[2:6], made[6:]

    kept, given, terms = call(
        late_kernel,
        [(PARTS, 8 * TILES, LANES)] * 2 + [(8, LANES)],
        [SMEM] + [VMEM] * 10,
        scratch_shapes=[pltpu.VMEM((4 * width, width), F32)] * 2,
    )(place, *grams, opp_a, opp_b, *image, st, ritz)

    payload = kept + shifted(given, "core", 1)
    got = lax.all_to_all(payload, RING, 0, 0, tiled=True)
    around = [shifted(terms, "col", by) for by in (1, 2, 3)]
    from_prev = shifted(part_after, "col", 1)
    from_next = shifted(part_before, "col", -1)
    from_opp = shifted(part_opp, "col", 2)
    new_modes, new_image = call(
        modes_kernel,
        [(modes, rows)] * 2,
        [SMEM] + [VMEM] * 10,
        scratch_shapes=[pltpu.VMEM((4 * modes, width), F32)],
    )(col, st, before, after, opp_a, opp_b, ritz, part_own, from_prev, from_next, from_opp)

    part = jnp.concatenate(
        [jnp.sum(got, axis=0), terms + around[0] + around[1] + around[2]], axis=0
    )
    part = jnp.broadcast_to(part[None], (4,) + part.shape)
    part = lax.all_to_all(part, "zh", 0, 0, tiled=True)
    part = jnp.sum(part, axis=0)
    parts = lax.all_to_all(spread_out(part), RING, 0, 0, tiled=True)
    others = shifted(parts, "core", 1)

    stiff, mass, theta, residual = call(
        final_kernel,
        [(width, 4 * width), (width, 4 * width), (1, modes), (modes, rows)],
        [SMEM] + [VMEM] * 4,
    )(place, parts, others, new_modes, new_image)
    return (new_modes.T, residual.T, theta[0], stiff.T, mass.T)


def solution(mesh):
    mesh = Mesh(mesh.devices.reshape(4, 2, 4, 2, 4), WIRE + ("col",))
    return jax.shard_map(
        shards,
        mesh=mesh,
        in_specs=(P(WIRE, "col"), P(WIRE, None), P(WIRE, None), P()),
        out_specs=(P(WIRE, "col"), P(WIRE, "col"), P("col"), P(None, "col"), P(None, "col")),
        check_vma=False,
    )
```

```python
import functools

import jax
import jax.numpy as jnp
from jax import lax
from jax.experimental import pallas as pl
from jax.experimental.pallas import tpu as pltpu
from jax.sharding import Mesh, PartitionSpec as P


RING = ("zl", "y", "core")
WIRE = ("zh", "zl", "y", "core")
BLOCK = 64
PARTS = 16
TILES = 5
PAIRS = 4
LANES = 128
F32 = jnp.float32
NN = (((1,), (0,)), ((), ()))
NT = (((1,), (1,)), ((), ()))
VMEM = pl.BlockSpec(memory_space=pltpu.VMEM)
SMEM = pl.BlockSpec(memory_space=pltpu.SMEM)


def shifted(array, axis, by):
    length = lax.axis_size(axis)
    return lax.ppermute(array, axis, [(i, (i + by) % length) for i in range(length)])


def to_sides(array, distance):
    length = lax.axis_size(WIRE)
    pairs = [((i - distance if i % 2 == 0 else i + distance) % length, i) for i in range(length)]
    return lax.ppermute(array, WIRE, pairs)


def split(x):
    high = x.astype(jnp.bfloat16)
    return high, (x - high.astype(F32)).astype(jnp.bfloat16)


def dot3(a, b, dims):
    (ah, al), (bh, bl) = a, b
    one = lambda x, y: lax.dot_general(x, y, dims, preferred_element_type=F32)
    rows = ah.shape[0]
    first = one(jnp.concatenate([ah, al], axis=0), bh)
    return first[:rows] + (first[rows:] + one(ah, bl))


def lane_tile(x):
    short = LANES - x.shape[0]
    return jnp.concatenate([x, jnp.zeros((short, x.shape[1]), x.dtype)], axis=0) if short else x


def dot4(a, b):
    both = lax.dot_general(
        jnp.concatenate(a, axis=0),
        jnp.concatenate([lane_tile(b[0]), lane_tile(b[1])], axis=0),
        NT,
        preferred_element_type=F32,
    )
    rows = a[0].shape[0]
    both = both[:rows] + both[rows:]
    return both[:, :LANES] + both[:, LANES:]


def low_half(shape):
    return lax.broadcasted_iota(jnp.int32, shape, 1) < BLOCK


def tile_at(ref, index):
    return ref[:, pl.ds(pl.multiple_of(index // 2 * LANES, LANES), LANES)]


def in_half(tile, index, half):
    return jnp.where(index % 2 == half, tile, pltpu.roll(tile, BLOCK, 1))


def group_start(here, by, blk, count):
    start = here + by * blk
    return jnp.where(start >= count, start - count, jnp.where(start < 0, start + count, start))


def image_kernel(
    count, col, cols, st, swap, near, relay, far, values, before, after, ritz,
    image_high, image_low, stiff, stiff_terms, mass, mass_terms,
    part_own, part_after, part_opp, part_before, stiff_sum, mass_sum, turned
):
    m = pl.program_id(0)
    width = st.shape[0]
    pairs = values.shape[0] // LANES
    left_half = low_half((width, LANES))
    flip = lambda x: pltpu.roll(x, BLOCK, 1)
    images, owns = [], []
    blk = cols.shape[1]
    here = cols[0, 0]
    even = here // blk % 2 == 0
    starts = [group_start(here, by, blk, count) for by in (1, 2, -1, -2)]
    sources = ((swap, near), (relay, far), (near, swap), (far, relay))

    @pl.when(m == 0)
    def _():
        stiff_sum[...] = jnp.zeros_like(stiff_sum)
        mass_sum[...] = jnp.zeros_like(mass_sum)
        turned[...] = ritz[pl.ds(pl.multiple_of(col[0] * width, 8), width), :].T

    modes = part_own.shape[0]
    send = split(
        jnp.concatenate(
            [turned[pl.ds(pl.multiple_of((col[0] + i) % 4 * modes, 8), modes), :] for i in range(4)], axis=0
        )
    )
    for h in range(pairs):
        tile = m * pairs + h
        own = st[:, pl.ds(pl.multiple_of(tile * LANES, LANES), LANES)]
        owns.append(own)
        left, right = [], []
        for q in range(2):
            row = 2 * tile + q
            index = cols[1, row] - here
            close = in_half(tile_at(st, index), index, 1 - q)
            first = jnp.where(left_half, own, close) if q == 0 else jnp.where(left_half, close, own)
            beyond = []
            for slot in range(2):
                index = cols[2 + slot, row] - starts[2 * q + slot]
                one, two = (tile_at(ref, index) for ref in sources[2 * q + slot])
                beyond.append(in_half(jnp.where(even, one, two), index, slot))
            left.append(jnp.concatenate([first, jnp.where(left_half, *beyond)], axis=1))
            coef = values[(2 * h + q) * BLOCK : (2 * h + q + 1) * BLOCK, :]
            if q:
                coef = jnp.concatenate([flip(coef[:, :LANES]), coef[:, LANES:]], axis=1)
            right.append(coef)
        part = dot4(split(jnp.concatenate(left, axis=0)), split(jnp.concatenate(right, axis=0)))
        images.append(split(4.0 * own + jnp.where(left_half, part[:width], part[width:])))
        if h % 2:
            span = slice((h - 1) * LANES, (h + 1) * LANES)
            image = tuple(jnp.concatenate([images[h - 1][i], images[h][i]], axis=1) for i in range(2))
            image_high[:, span], image_low[:, span] = image
            mine = jnp.concatenate(owns[h - 1 :], axis=1)
            pieces = split(jnp.concatenate([mine, before[:, span], after[:, span]], axis=0))
            mass_sum[...] += dot4(pieces, (pieces[0][:width], pieces[1][:width]))
            stiff_sum[...] += dot4(pieces, image)
            part = dot3(send, image, NN)
            for i, out in enumerate((part_own, part_after, part_opp, part_before)):
                out[:, span] = part[i * modes : (i + 1) * modes]

    @pl.when(m == pl.num_programs(0) - 1)
    def _():
        for gram, terms, total in ((stiff, stiff_terms, stiff_sum), (mass, mass_terms, mass_sum)):
            for i in range(3):
                gram[i] = total[i * width : (i + 1) * width, :width]
            piece_terms(gram, col[0], ritz, terms)


def quotient_terms(piece, mine, ritz, start):
    left = dot3(split(piece), split(mine), NN)
    return jnp.sum(left * ritz[pl.ds(start, piece.shape[0]), :], axis=0, keepdims=True)


def piece_terms(gram, c, ritz, terms):
    width = gram.shape[1]
    at = lambda by: pl.multiple_of((c + by) % 4 * width, 8)
    mine = ritz[pl.ds(at(0), width), :]
    total = quotient_terms(gram[0], mine, ritz, at(0))
    total = total + quotient_terms(gram[1], mine, ritz, at(3))
    terms[...] = total + quotient_terms(gram[2], mine, ritz, at(1))


def late_kernel(
    col, stiff3, stiff_terms, mass3, mass_terms, opp_a, opp_b, image_high, image_low, st, ritz,
    payload, terms, stiff, mass
):
    c = col[0]
    width = st.shape[0]
    far = split(jnp.concatenate([opp_a[...], opp_b[...]], axis=0))
    far_stiff = dot4(far, (image_high[...], image_low[...]))[:, :width]
    far_mass = dot4(far, split(st[...]))[:, :width]
    terms[...] = jnp.zeros_like(terms)
    at = lambda by: pl.multiple_of((c + by) % 4 * width, 8)
    mine = ritz[pl.ds(at(0), width), :]
    turned = []
    for i, (block, whole, pieces, sums) in enumerate(
        (
            (far_stiff, stiff, stiff3, stiff_terms),
            (far_mass, mass, mass3, mass_terms),
        )
    ):
        for piece, by in ((pieces[0], 0), (pieces[1], 3), (pieces[2], 1), (block, 2)):
            whole[pl.ds(at(by), width), :] = piece
        terms[i : i + 1, :] = sums[...] + quotient_terms(block, mine, ritz, at(2))
        turned.append(whole[...].T)
    for t in range(PARTS * TILES):
        k, to = t // TILES, t % TILES * 8
        i, j = t // 3 * 8, t % 3 * LANES
        if i < 2 * width:
            payload[k, to : to + 8, :] = turned[i // width][i % width : i % width + 8, j : j + LANES]
        else:
            payload[k, to : to + 8, :] = jnp.zeros((8, LANES), F32)


def modes_kernel(
    col, st, before, after, opp_a, opp_b, ritz, own, from_prev, from_next, from_opp, modes, image, turned
):
    width = st.shape[0]
    coef = []
    for by in (0, 3, 1, 2):
        turned[...] = ritz[pl.ds(pl.multiple_of((col[0] + by) % 4 * width, 8), width), :].T
        coef.append(turned[pl.ds(pl.multiple_of(col[0] * modes.shape[0], 8), modes.shape[0]), :])
    opp = jnp.concatenate([opp_a[...], opp_b[...]], axis=0)
    modes[...] = (
        dot3(split(coef[0]), split(st[...]), NN)
        + dot3(split(coef[1]), split(before[...]), NN)
        + dot3(split(coef[2]), split(after[...]), NN)
        + dot3(split(coef[3]), split(opp), NN)
    )
    image[...] = (own[...] + from_opp[...]) + (from_prev[...] + from_next[...])


def final_kernel(col, parts, modes, image, stiff, mass, theta, residual):
    total = jnp.float32(196608.0)
    terms = parts[0, 8 * TILES :, :]
    for k in range(1, PARTS):
        terms = terms + parts[k, 8 * TILES :, :]
    quotient = terms[0:1, :] / terms[1:2, :]
    shape = (modes.shape[0], LANES)
    here = lax.broadcasted_iota(jnp.int32, shape, 1) == (
        lax.broadcasted_iota(jnp.int32, shape, 0) + col[0] * shape[0]
    )
    column = jnp.sum(jnp.where(here, jnp.broadcast_to(quotient, shape), 0.0), axis=1, keepdims=True)
    theta[...] = pltpu.roll(
        jnp.broadcast_to(quotient, (8, LANES)), (4 - col[0]) % 4 * shape[0], 1
    )[0:1, : shape[0]]
    residual[...] = image[...] - column * modes[...]
    width = stiff.shape[0]
    for t in range(2 * width // 8 * 3):
        k, at = t // TILES, t % TILES * 8
        i, j = t // 3 * 8, t % 3 * LANES
        out = stiff if i < width else mass
        out[i % width : i % width + 8, j : j + LANES] = parts[k, at : at + 8, :] / total


def call(kernel, shapes, in_specs, dtypes=None, **kwargs):
    dtypes = dtypes or [F32] * len(shapes)
    return pl.pallas_call(
        kernel,
        out_shape=[jax.ShapeDtypeStruct(s, d) for s, d in zip(shapes, dtypes)],
        in_specs=in_specs,
        out_specs=kwargs.pop("out_specs", [VMEM] * len(shapes)),
        **kwargs,
    )


def spread_out(part):
    return jnp.broadcast_to(part[None], (PARTS,) + part.shape)


def shards(search, values, block_cols, ritz):
    rows, width = search.shape
    blk = block_cols.shape[0]
    modes = ritz.shape[1] // 4
    half = width // 2
    c = lax.axis_index("col")
    groups = lax.axis_size(WIRE)
    col = jnp.reshape(c, (1,)).astype(jnp.int32)
    st = search.T
    cols = block_cols.T

    before = shifted(st, "col", 1)
    after = shifted(st, "col", -1)
    near = to_sides(st, 1)
    far = to_sides(st, 2)
    swap = shifted(st, "core", 1)
    relay = shifted(near, "core", 1)

    opp_a = shifted(before[:half], "col", 1)
    opp_b = shifted(after[half:], "col", -1)

    tile = lambda n: pl.BlockSpec((width, n), lambda m: (0, m))
    whole = pl.BlockSpec((width, rows), lambda m: (0, 0))
    step_lanes = PAIRS * LANES
    grams = [(3, width, width), (1, LANES)] * 2
    gram_specs = [pl.BlockSpec((3, width, width), lambda m: (0, 0, 0)), pl.BlockSpec((1, LANES), lambda m: (0, 0))] * 2
    made = call(
        functools.partial(image_kernel, blk * groups),
        [(width, rows)] * 2 + grams + [(modes, rows)] * 4,
        [SMEM] * 2
        + [whole] * 5
        + [pl.BlockSpec((step_lanes, values.shape[1]), lambda m: (m, 0))]
        + [tile(step_lanes)] * 2
        + [VMEM],
        [jnp.bfloat16] * 2 + [F32] * 8,
        out_specs=[tile(step_lanes)] * 2
        + gram_specs
        + [pl.BlockSpec((modes, step_lanes), lambda m: (0, m))] * 4,
        grid=(rows // step_lanes,),
        scratch_shapes=[pltpu.VMEM((3 * width, LANES), F32)] * 2 + [pltpu.VMEM((4 * modes, width), F32)],
    )(col, cols, st, swap, near, relay, far, values, before, after, ritz)
    image, grams, (part_own, part_after, part_opp, part_before) = made[:2], made[2:6], made[6:]

    payload, terms = call(
        late_kernel,
        [(PARTS, 8 * TILES, LANES), (8, LANES)],
        [SMEM] + [VMEM] * 10,
        scratch_shapes=[pltpu.VMEM((4 * width, width), F32)] * 2,
    )(col, *grams, opp_a, opp_b, *image, st, ritz)

    got = lax.all_to_all(payload, RING, 0, 0, tiled=True)
    around = [shifted(terms, "col", by) for by in (1, 2, 3)]
    from_prev = shifted(part_after, "col", 1)
    from_next = shifted(part_before, "col", -1)
    from_opp = shifted(part_opp, "col", 2)
    new_modes, new_image = call(
        modes_kernel,
        [(modes, rows)] * 2,
        [SMEM] + [VMEM] * 10,
        scratch_shapes=[pltpu.VMEM((4 * modes, width), F32)],
    )(col, st, before, after, opp_a, opp_b, ritz, part_own, from_prev, from_next, from_opp)

    part = jnp.concatenate(
        [jnp.sum(got, axis=0), terms + around[0] + around[1] + around[2]], axis=0
    )
    part = jnp.broadcast_to(part[None], (4,) + part.shape)
    part = lax.all_to_all(part, "zh", 0, 0, tiled=True)
    part = jnp.sum(part, axis=0)
    parts = lax.all_to_all(spread_out(part), RING, 0, 0, tiled=True)

    stiff, mass, theta, residual = call(
        final_kernel,
        [(width, 4 * width), (width, 4 * width), (1, modes), (modes, rows)],
        [SMEM] + [VMEM] * 3,
    )(col, parts, new_modes, new_image)
    return (new_modes.T, residual.T, theta[0], stiff.T, mass.T)


def solution(mesh):
    mesh = Mesh(mesh.devices.reshape(4, 2, 4, 2, 4), WIRE + ("col",))
    return jax.shard_map(
        shards,
        mesh=mesh,
        in_specs=(P(WIRE, "col"), P(WIRE, None), P(WIRE, None), P()),
        out_specs=(P(WIRE, "col"), P(WIRE, "col"), P("col"), P(None, "col"), P(None, "col")),
        check_vma=False,
    )
```

```python
import functools

import jax
import jax.numpy as jnp
from jax import lax
from jax.experimental import pallas as pl
from jax.experimental.pallas import tpu as pltpu
from jax.sharding import Mesh, PartitionSpec as P


RING = ("zl", "y", "core")
WIRE = ("zh", "zl", "y", "core")
BLOCK = 64
PARTS = 16
TILES = 5
PAIRS = 4
LANES = 128
F32 = jnp.float32
NN = (((1,), (0,)), ((), ()))
NT = (((1,), (1,)), ((), ()))
VMEM = pl.BlockSpec(memory_space=pltpu.VMEM)
SMEM = pl.BlockSpec(memory_space=pltpu.SMEM)
HBM = pl.BlockSpec(memory_space=pltpu.HBM)


def shifted(array, axis, by):
    length = lax.axis_size(axis)
    return lax.ppermute(array, axis, [(i, (i + by) % length) for i in range(length)])


def to_sides(array, distance):
    length = lax.axis_size(WIRE)
    pairs = [((i - distance if i % 2 == 0 else i + distance) % length, i) for i in range(length)]
    return lax.ppermute(array, WIRE, pairs)


def split(x):
    high = x.astype(jnp.bfloat16)
    return high, (x - high.astype(F32)).astype(jnp.bfloat16)


def dot3(a, b, dims):
    (ah, al), (bh, bl) = a, b
    one = lambda x, y: lax.dot_general(x, y, dims, preferred_element_type=F32)
    rows = ah.shape[0]
    first = one(jnp.concatenate([ah, al], axis=0), bh)
    return first[:rows] + (first[rows:] + one(ah, bl))


def lane_tile(x):
    short = LANES - x.shape[0]
    return jnp.concatenate([x, jnp.zeros((short, x.shape[1]), x.dtype)], axis=0) if short else x


def dot4(a, b):
    both = lax.dot_general(
        jnp.concatenate(a, axis=0),
        jnp.concatenate([lane_tile(b[0]), lane_tile(b[1])], axis=0),
        NT,
        preferred_element_type=F32,
    )
    rows = a[0].shape[0]
    both = both[:rows] + both[rows:]
    return both[:, :LANES] + both[:, LANES:]


def low_half(shape):
    return lax.broadcasted_iota(jnp.int32, shape, 1) < BLOCK


def tile_at(ref, index):
    return ref[:, pl.ds(pl.multiple_of(index // 2 * LANES, LANES), LANES)]


def in_half(tile, index, half):
    return jnp.where(index % 2 == half, tile, pltpu.roll(tile, BLOCK, 1))


def group_start(here, by, blk, count):
    start = here + by * blk
    return jnp.where(start >= count, start - count, jnp.where(start < 0, start + count, start))


def image_kernel(
    count, col, cols, st, swap, near, relay, far, values, before, after, ritz,
    image_high, image_low, stiff, stiff_terms, mass, mass_terms,
    part_own, part_after, part_opp, part_before, stiff_sum, mass_sum, turned, beside, sems
):
    m = pl.program_id(0)
    width = st.shape[0]
    pairs = values.shape[0] // LANES
    left_half = low_half((width, LANES))
    flip = lambda x: pltpu.roll(x, BLOCK, 1)
    images, owns = [], []
    blk = cols.shape[1]
    here = cols[0, 0]
    starts = [group_start(here, by, blk, count) for by in (1, 2, -1, -2)]

    @pl.when(m == 0)
    def _():
        stiff_sum[...] = jnp.zeros_like(stiff_sum)
        mass_sum[...] = jnp.zeros_like(mass_sum)
        odd = here // blk % 2
        copies = [
            pltpu.make_async_copy(source, beside.at[slot], sems.at[i])
            for i, (source, slot) in enumerate(
                ((swap, 2 * odd), (near, 2 - 2 * odd), (relay, 1 + 2 * odd), (far, 3 - 2 * odd))
            )
        ]
        for copy in copies:
            copy.start()
        for copy in copies:
            copy.wait()
        turned[...] = ritz[pl.ds(pl.multiple_of(col[0] * width, 8), width), :].T

    modes = part_own.shape[0]
    send = split(
        jnp.concatenate(
            [turned[pl.ds(pl.multiple_of((col[0] + i) % 4 * modes, 8), modes), :] for i in range(4)], axis=0
        )
    )
    for h in range(pairs):
        tile = m * pairs + h
        own = st[:, pl.ds(pl.multiple_of(tile * LANES, LANES), LANES)]
        owns.append(own)
        left, right = [], []
        for q in range(2):
            row = 2 * tile + q
            index = cols[1, row] - here
            close = in_half(tile_at(st, index), index, 1 - q)
            first = jnp.where(left_half, own, close) if q == 0 else jnp.where(left_half, close, own)
            beyond = []
            for slot in range(2):
                index = cols[2 + slot, row] - starts[2 * q + slot]
                beyond.append(in_half(tile_at(beside.at[2 * q + slot], index), index, slot))
            left.append(jnp.concatenate([first, jnp.where(left_half, *beyond)], axis=1))
            coef = values[(2 * h + q) * BLOCK : (2 * h + q + 1) * BLOCK, :]
            if q:
                coef = jnp.concatenate([flip(coef[:, :LANES]), coef[:, LANES:]], axis=1)
            right.append(coef)
        part = dot4(split(jnp.concatenate(left, axis=0)), split(jnp.concatenate(right, axis=0)))
        images.append(split(4.0 * own + jnp.where(left_half, part[:width], part[width:])))
        if h % 2:
            span = slice((h - 1) * LANES, (h + 1) * LANES)
            image = tuple(jnp.concatenate([images[h - 1][i], images[h][i]], axis=1) for i in range(2))
            image_high[:, span], image_low[:, span] = image
            mine = jnp.concatenate(owns[h - 1 :], axis=1)
            pieces = split(jnp.concatenate([mine, before[:, span], after[:, span]], axis=0))
            mass_sum[...] += dot4(pieces, (pieces[0][:width], pieces[1][:width]))
            stiff_sum[...] += dot4(pieces, image)
            part = dot3(send, image, NN)
            for i, out in enumerate((part_own, part_after, part_opp, part_before)):
                out[:, span] = part[i * modes : (i + 1) * modes]

    @pl.when(m == pl.num_programs(0) - 1)
    def _():
        for gram, terms, total in ((stiff, stiff_terms, stiff_sum), (mass, mass_terms, mass_sum)):
            for i in range(3):
                gram[i] = total[i * width : (i + 1) * width, :width]
            piece_terms(gram, col[0], ritz, terms)


def quotient_terms(piece, mine, ritz, start):
    left = dot3(split(piece), split(mine), NN)
    return jnp.sum(left * ritz[pl.ds(start, piece.shape[0]), :], axis=0, keepdims=True)


def piece_terms(gram, c, ritz, terms):
    width = gram.shape[1]
    at = lambda by: pl.multiple_of((c + by) % 4 * width, 8)
    mine = ritz[pl.ds(at(0), width), :]
    total = quotient_terms(gram[0], mine, ritz, at(0))
    total = total + quotient_terms(gram[1], mine, ritz, at(3))
    terms[...] = total + quotient_terms(gram[2], mine, ritz, at(1))


def late_kernel(
    col, stiff3, stiff_terms, mass3, mass_terms, opp_a, opp_b, image_high, image_low, st, ritz,
    payload, terms, stiff, mass
):
    c = col[0]
    width = st.shape[0]
    far = split(jnp.concatenate([opp_a[...], opp_b[...]], axis=0))
    far_stiff = dot4(far, (image_high[...], image_low[...]))[:, :width]
    far_mass = dot4(far, split(st[...]))[:, :width]
    terms[...] = jnp.zeros_like(terms)
    at = lambda by: pl.multiple_of((c + by) % 4 * width, 8)
    mine = ritz[pl.ds(at(0), width), :]
    turned = []
    for i, (block, whole, pieces, sums) in enumerate(
        (
            (far_stiff, stiff, stiff3, stiff_terms),
            (far_mass, mass, mass3, mass_terms),
        )
    ):
        for piece, by in ((pieces[0], 0), (pieces[1], 3), (pieces[2], 1), (block, 2)):
            whole[pl.ds(at(by), width), :] = piece
        terms[i : i + 1, :] = sums[...] + quotient_terms(block, mine, ritz, at(2))
        turned.append(whole[...].T)
    for t in range(PARTS * TILES):
        k, to = t // TILES, t % TILES * 8
        i, j = t // 3 * 8, t % 3 * LANES
        if i < 2 * width:
            payload[k, to : to + 8, :] = turned[i // width][i % width : i % width + 8, j : j + LANES]
        else:
            payload[k, to : to + 8, :] = jnp.zeros((8, LANES), F32)


def modes_kernel(
    col, st, before, after, opp_a, opp_b, ritz, own, from_prev, from_next, from_opp, modes, image, turned
):
    width = st.shape[0]
    coef = []
    for by in (0, 3, 1, 2):
        turned[...] = ritz[pl.ds(pl.multiple_of((col[0] + by) % 4 * width, 8), width), :].T
        coef.append(turned[pl.ds(pl.multiple_of(col[0] * modes.shape[0], 8), modes.shape[0]), :])
    opp = jnp.concatenate([opp_a[...], opp_b[...]], axis=0)
    modes[...] = (
        dot3(split(coef[0]), split(st[...]), NN)
        + dot3(split(coef[1]), split(before[...]), NN)
        + dot3(split(coef[2]), split(after[...]), NN)
        + dot3(split(coef[3]), split(opp), NN)
    )
    image[...] = (own[...] + from_opp[...]) + (from_prev[...] + from_next[...])


def final_kernel(col, parts, modes, image, stiff, mass, theta, residual):
    total = jnp.float32(196608.0)
    terms = parts[0, 8 * TILES :, :]
    for k in range(1, PARTS):
        terms = terms + parts[k, 8 * TILES :, :]
    quotient = terms[0:1, :] / terms[1:2, :]
    shape = (modes.shape[0], LANES)
    here = lax.broadcasted_iota(jnp.int32, shape, 1) == (
        lax.broadcasted_iota(jnp.int32, shape, 0) + col[0] * shape[0]
    )
    column = jnp.sum(jnp.where(here, jnp.broadcast_to(quotient, shape), 0.0), axis=1, keepdims=True)
    theta[...] = pltpu.roll(
        jnp.broadcast_to(quotient, (8, LANES)), (4 - col[0]) % 4 * shape[0], 1
    )[0:1, : shape[0]]
    residual[...] = image[...] - column * modes[...]
    width = stiff.shape[0]
    for t in range(2 * width // 8 * 3):
        k, at = t // TILES, t % TILES * 8
        i, j = t // 3 * 8, t % 3 * LANES
        out = stiff if i < width else mass
        out[i % width : i % width + 8, j : j + LANES] = parts[k, at : at + 8, :] / total


def call(kernel, shapes, in_specs, dtypes=None, **kwargs):
    dtypes = dtypes or [F32] * len(shapes)
    return pl.pallas_call(
        kernel,
        out_shape=[jax.ShapeDtypeStruct(s, d) for s, d in zip(shapes, dtypes)],
        in_specs=in_specs,
        out_specs=kwargs.pop("out_specs", [VMEM] * len(shapes)),
        **kwargs,
    )


def spread_out(part):
    return jnp.broadcast_to(part[None], (PARTS,) + part.shape)


def shards(search, values, block_cols, ritz):
    rows, width = search.shape
    blk = block_cols.shape[0]
    modes = ritz.shape[1] // 4
    half = width // 2
    c = lax.axis_index("col")
    groups = lax.axis_size(WIRE)
    col = jnp.reshape(c, (1,)).astype(jnp.int32)
    st = search.T
    cols = block_cols.T

    before = shifted(st, "col", 1)
    after = shifted(st, "col", -1)
    near = to_sides(st, 1)
    far = to_sides(st, 2)
    swap = shifted(st, "core", 1)
    relay = shifted(near, "core", 1)

    opp_a = shifted(before[:half], "col", 1)
    opp_b = shifted(after[half:], "col", -1)

    tile = lambda n: pl.BlockSpec((width, n), lambda m: (0, m))
    whole = pl.BlockSpec((width, rows), lambda m: (0, 0))
    step_lanes = PAIRS * LANES
    grams = [(3, width, width), (1, LANES)] * 2
    gram_specs = [pl.BlockSpec((3, width, width), lambda m: (0, 0, 0)), pl.BlockSpec((1, LANES), lambda m: (0, 0))] * 2
    made = call(
        functools.partial(image_kernel, blk * groups),
        [(width, rows)] * 2 + grams + [(modes, rows)] * 4,
        [SMEM] * 2
        + [whole]
        + [HBM] * 4
        + [pl.BlockSpec((step_lanes, values.shape[1]), lambda m: (m, 0))]
        + [tile(step_lanes)] * 2
        + [VMEM],
        [jnp.bfloat16] * 2 + [F32] * 8,
        out_specs=[tile(step_lanes)] * 2
        + gram_specs
        + [pl.BlockSpec((modes, step_lanes), lambda m: (0, m))] * 4,
        grid=(rows // step_lanes,),
        scratch_shapes=[pltpu.VMEM((3 * width, LANES), F32)] * 2
        + [
            pltpu.VMEM((4 * modes, width), F32),
            pltpu.VMEM((4, width, rows), F32),
            pltpu.SemaphoreType.DMA((4,)),
        ],
    )(col, cols, st, swap, near, relay, far, values, before, after, ritz)
    image, grams, (part_own, part_after, part_opp, part_before) = made[:2], made[2:6], made[6:]

    payload, terms = call(
        late_kernel,
        [(PARTS, 8 * TILES, LANES), (8, LANES)],
        [SMEM] + [VMEM] * 10,
        scratch_shapes=[pltpu.VMEM((4 * width, width), F32)] * 2,
    )(col, *grams, opp_a, opp_b, *image, st, ritz)

    got = lax.all_to_all(payload, RING, 0, 0, tiled=True)
    around = [shifted(terms, "col", by) for by in (1, 2, 3)]
    from_prev = shifted(part_after, "col", 1)
    from_next = shifted(part_before, "col", -1)
    from_opp = shifted(part_opp, "col", 2)
    new_modes, new_image = call(
        modes_kernel,
        [(modes, rows)] * 2,
        [SMEM] + [VMEM] * 10,
        scratch_shapes=[pltpu.VMEM((4 * modes, width), F32)],
    )(col, st, before, after, opp_a, opp_b, ritz, part_own, from_prev, from_next, from_opp)

    part = jnp.concatenate(
        [jnp.sum(got, axis=0), terms + around[0] + around[1] + around[2]], axis=0
    )
    part = jnp.broadcast_to(part[None], (4,) + part.shape)
    part = lax.all_to_all(part, "zh", 0, 0, tiled=True)
    part = jnp.sum(part, axis=0)
    parts = lax.all_to_all(spread_out(part), RING, 0, 0, tiled=True)

    stiff, mass, theta, residual = call(
        final_kernel,
        [(width, 4 * width), (width, 4 * width), (1, modes), (modes, rows)],
        [SMEM] + [VMEM] * 3,
    )(col, parts, new_modes, new_image)
    return (new_modes.T, residual.T, theta[0], stiff.T, mass.T)


def solution(mesh):
    mesh = Mesh(mesh.devices.reshape(4, 2, 4, 2, 4), WIRE + ("col",))
    return jax.shard_map(
        shards,
        mesh=mesh,
        in_specs=(P(WIRE, "col"), P(WIRE, None), P(WIRE, None), P()),
        out_specs=(P(WIRE, "col"), P(WIRE, "col"), P("col"), P(None, "col"), P(None, "col")),
        check_vma=False,
    )
```

```python
import functools

import jax
import jax.numpy as jnp
from jax import lax
from jax.experimental import pallas as pl
from jax.experimental.pallas import tpu as pltpu
from jax.sharding import Mesh, PartitionSpec as P


RING = ("zl", "y", "core")
WIRE = ("zh", "zl", "y", "core")
BLOCK = 64
PARTS = 16
TILES = 5
PAIRS = 4
LANES = 128
F32 = jnp.float32
NN = (((1,), (0,)), ((), ()))
NT = (((1,), (1,)), ((), ()))
VMEM = pl.BlockSpec(memory_space=pltpu.VMEM)
SMEM = pl.BlockSpec(memory_space=pltpu.SMEM)


def shifted(array, axis, by):
    length = lax.axis_size(axis)
    return lax.ppermute(array, axis, [(i, (i + by) % length) for i in range(length)])


def to_sides(array, distance, back=False):
    length = lax.axis_size(WIRE)
    pairs = [((i - distance if i % 2 == 0 else i + distance) % length, i) for i in range(length)]
    return lax.ppermute(array, WIRE, [pair[::-1] for pair in pairs] if back else pairs)


def split(x):
    high = x.astype(jnp.bfloat16)
    return high, (x - high.astype(F32)).astype(jnp.bfloat16)


def dot3(a, b, dims):
    (ah, al), (bh, bl) = a, b
    one = lambda x, y: lax.dot_general(x, y, dims, preferred_element_type=F32)
    rows = ah.shape[0]
    first = one(jnp.concatenate([ah, al], axis=0), bh)
    return first[:rows] + (first[rows:] + one(ah, bl))


def lane_tile(x):
    short = LANES - x.shape[0]
    return jnp.concatenate([x, jnp.zeros((short, x.shape[1]), x.dtype)], axis=0) if short else x


def dot4(a, b):
    both = lax.dot_general(
        jnp.concatenate(a, axis=0),
        jnp.concatenate([lane_tile(b[0]), lane_tile(b[1])], axis=0),
        NT,
        preferred_element_type=F32,
    )
    rows = a[0].shape[0]
    both = both[:rows] + both[rows:]
    return both[:, :LANES] + both[:, LANES:]


def low_half(shape):
    return lax.broadcasted_iota(jnp.int32, shape, 1) < BLOCK


def tile_at(ref, index):
    return ref[:, pl.ds(pl.multiple_of(index // 2 * LANES, LANES), LANES)]


def in_half(tile, index, half):
    return jnp.where(index % 2 == half, tile, pltpu.roll(tile, BLOCK, 1))


def group_start(here, by, blk, count):
    start = here + by * blk
    return jnp.where(start >= count, start - count, jnp.where(start < 0, start + count, start))


def pack_kernel(cols, asked, st, packed):
    low = low_half((st.shape[0], LANES))
    here = cols[0, 0]
    parity = 1 - here // cols.shape[1] % 2

    def step(m, carry):
        first = asked[3, 4 * m + parity] - here
        second = asked[3, 4 * m + 2 + parity] - here
        packed[:, pl.ds(pl.multiple_of(m * LANES, LANES), LANES)] = jnp.where(
            low, in_half(tile_at(st, first), first, 0), in_half(tile_at(st, second), second, 1)
        )
        return carry

    lax.fori_loop(0, packed.shape[1] // LANES, step, 0, unroll=4)


def image_kernel(
    count, col, cols, st, swap, near, relay, far, values, before, after, ritz,
    image_high, image_low, stiff, stiff_terms, mass, mass_terms,
    part_own, part_after, part_opp, part_before, stiff_sum, mass_sum, turned
):
    m = pl.program_id(0)
    width = st.shape[0]
    pairs = values.shape[0] // LANES
    left_half = low_half((width, LANES))
    flip = lambda x: pltpu.roll(x, BLOCK, 1)
    images, owns = [], []
    blk = cols.shape[1]
    here = cols[0, 0]
    even = here // blk % 2 == 0
    starts = [group_start(here, by, blk, count) for by in (1, 2, -1, -2)]
    beside = ((swap, near), (near, swap))

    @pl.when(m == 0)
    def _():
        stiff_sum[...] = jnp.zeros_like(stiff_sum)
        mass_sum[...] = jnp.zeros_like(mass_sum)
        turned[...] = ritz[pl.ds(pl.multiple_of(col[0] * width, 8), width), :].T

    modes = part_own.shape[0]
    send = split(
        jnp.concatenate(
            [turned[pl.ds(pl.multiple_of((col[0] + i) % 4 * modes, 8), modes), :] for i in range(4)], axis=0
        )
    )
    for h in range(pairs):
        tile = m * pairs + h
        own = st[:, pl.ds(pl.multiple_of(tile * LANES, LANES), LANES)]
        owns.append(own)
        left, right = [], []
        for q in range(2):
            row = 2 * tile + q
            index = cols[1, row] - here
            close = in_half(tile_at(st, index), index, 1 - q)
            first = jnp.where(left_half, own, close) if q == 0 else jnp.where(left_half, close, own)
            index = cols[2, row] - starts[2 * q]
            one, two = (tile_at(ref, index) for ref in beside[q])
            third = in_half(jnp.where(even, one, two), index, 0)
            whole = even if q == 0 else jnp.logical_not(even)
            index = jnp.where(whole, cols[3, row] - starts[2 * q + 1], row // 2)
            last = tile_at(far, row // 2)
            last = jnp.where(whole, tile_at(relay, jnp.where(whole, index, 0)), last)
            beyond = (third, in_half(last, index, 1))
            left.append(jnp.concatenate([first, jnp.where(left_half, *beyond)], axis=1))
            coef = values[(2 * h + q) * BLOCK : (2 * h + q + 1) * BLOCK, :]
            if q:
                coef = jnp.concatenate([flip(coef[:, :LANES]), coef[:, LANES:]], axis=1)
            right.append(coef)
        part = dot4(split(jnp.concatenate(left, axis=0)), split(jnp.concatenate(right, axis=0)))
        images.append(split(4.0 * own + jnp.where(left_half, part[:width], part[width:])))
        if h % 2:
            span = slice((h - 1) * LANES, (h + 1) * LANES)
            image = tuple(jnp.concatenate([images[h - 1][i], images[h][i]], axis=1) for i in range(2))
            image_high[:, span], image_low[:, span] = image
            mine = jnp.concatenate(owns[h - 1 :], axis=1)
            pieces = split(jnp.concatenate([mine, before[:, span], after[:, span]], axis=0))
            mass_sum[...] += dot4(pieces, (pieces[0][:width], pieces[1][:width]))
            stiff_sum[...] += dot4(pieces, image)
            part = dot3(send, image, NN)
            for i, out in enumerate((part_own, part_after, part_opp, part_before)):
                out[:, span] = part[i * modes : (i + 1) * modes]

    @pl.when(m == pl.num_programs(0) - 1)
    def _():
        for gram, terms, total in ((stiff, stiff_terms, stiff_sum), (mass, mass_terms, mass_sum)):
            for i in range(3):
                gram[i] = total[i * width : (i + 1) * width, :width]
            piece_terms(gram, col[0], ritz, terms)


def quotient_terms(piece, mine, ritz, start):
    left = dot3(split(piece), split(mine), NN)
    return jnp.sum(left * ritz[pl.ds(start, piece.shape[0]), :], axis=0, keepdims=True)


def piece_terms(gram, c, ritz, terms):
    width = gram.shape[1]
    at = lambda by: pl.multiple_of((c + by) % 4 * width, 8)
    mine = ritz[pl.ds(at(0), width), :]
    total = quotient_terms(gram[0], mine, ritz, at(0))
    total = total + quotient_terms(gram[1], mine, ritz, at(3))
    terms[...] = total + quotient_terms(gram[2], mine, ritz, at(1))


def late_kernel(
    col, stiff3, stiff_terms, mass3, mass_terms, opp_a, opp_b, image_high, image_low, st, ritz,
    payload, terms, stiff, mass
):
    c = col[0]
    width = st.shape[0]
    far = split(jnp.concatenate([opp_a[...], opp_b[...]], axis=0))
    far_stiff = dot4(far, (image_high[...], image_low[...]))[:, :width]
    far_mass = dot4(far, split(st[...]))[:, :width]
    terms[...] = jnp.zeros_like(terms)
    at = lambda by: pl.multiple_of((c + by) % 4 * width, 8)
    mine = ritz[pl.ds(at(0), width), :]
    turned = []
    for i, (block, whole, pieces, sums) in enumerate(
        (
            (far_stiff, stiff, stiff3, stiff_terms),
            (far_mass, mass, mass3, mass_terms),
        )
    ):
        for piece, by in ((pieces[0], 0), (pieces[1], 3), (pieces[2], 1), (block, 2)):
            whole[pl.ds(at(by), width), :] = piece
        terms[i : i + 1, :] = sums[...] + quotient_terms(block, mine, ritz, at(2))
        turned.append(whole[...].T)
    for t in range(PARTS * TILES):
        k, to = t // TILES, t % TILES * 8
        i, j = t // 3 * 8, t % 3 * LANES
        if i < 2 * width:
            payload[k, to : to + 8, :] = turned[i // width][i % width : i % width + 8, j : j + LANES]
        else:
            payload[k, to : to + 8, :] = jnp.zeros((8, LANES), F32)


def modes_kernel(
    col, st, before, after, opp_a, opp_b, ritz, own, from_prev, from_next, from_opp, modes, image, turned
):
    width = st.shape[0]
    coef = []
    for by in (0, 3, 1, 2):
        turned[...] = ritz[pl.ds(pl.multiple_of((col[0] + by) % 4 * width, 8), width), :].T
        coef.append(turned[pl.ds(pl.multiple_of(col[0] * modes.shape[0], 8), modes.shape[0]), :])
    opp = jnp.concatenate([opp_a[...], opp_b[...]], axis=0)
    modes[...] = (
        dot3(split(coef[0]), split(st[...]), NN)
        + dot3(split(coef[1]), split(before[...]), NN)
        + dot3(split(coef[2]), split(after[...]), NN)
        + dot3(split(coef[3]), split(opp), NN)
    )
    image[...] = (own[...] + from_opp[...]) + (from_prev[...] + from_next[...])


def final_kernel(col, parts, modes, image, stiff, mass, theta, residual):
    total = jnp.float32(196608.0)
    terms = parts[0, 8 * TILES :, :]
    for k in range(1, PARTS):
        terms = terms + parts[k, 8 * TILES :, :]
    quotient = terms[0:1, :] / terms[1:2, :]
    shape = (modes.shape[0], LANES)
    here = lax.broadcasted_iota(jnp.int32, shape, 1) == (
        lax.broadcasted_iota(jnp.int32, shape, 0) + col[0] * shape[0]
    )
    column = jnp.sum(jnp.where(here, jnp.broadcast_to(quotient, shape), 0.0), axis=1, keepdims=True)
    theta[...] = pltpu.roll(
        jnp.broadcast_to(quotient, (8, LANES)), (4 - col[0]) % 4 * shape[0], 1
    )[0:1, : shape[0]]
    residual[...] = image[...] - column * modes[...]
    width = stiff.shape[0]
    for t in range(2 * width // 8 * 3):
        k, at = t // TILES, t % TILES * 8
        i, j = t // 3 * 8, t % 3 * LANES
        out = stiff if i < width else mass
        out[i % width : i % width + 8, j : j + LANES] = parts[k, at : at + 8, :] / total


def call(kernel, shapes, in_specs, dtypes=None, **kwargs):
    dtypes = dtypes or [F32] * len(shapes)
    return pl.pallas_call(
        kernel,
        out_shape=[jax.ShapeDtypeStruct(s, d) for s, d in zip(shapes, dtypes)],
        in_specs=in_specs,
        out_specs=kwargs.pop("out_specs", [VMEM] * len(shapes)),
        **kwargs,
    )


def spread_out(part):
    return jnp.broadcast_to(part[None], (PARTS,) + part.shape)


def shards(search, values, block_cols, ritz):
    rows, width = search.shape
    blk = block_cols.shape[0]
    modes = ritz.shape[1] // 4
    half = width // 2
    c = lax.axis_index("col")
    groups = lax.axis_size(WIRE)
    col = jnp.reshape(c, (1,)).astype(jnp.int32)
    st = search.T
    cols = block_cols.T

    before = shifted(st, "col", 1)
    after = shifted(st, "col", -1)
    asked = to_sides(cols, 2, back=True)
    near = to_sides(st, 1)
    swap = shifted(st, "core", 1)
    packed = call(pack_kernel, [(width, rows // 2)], [SMEM] * 2 + [VMEM])(cols, asked, st)[0]
    far = to_sides(packed, 2)
    relay = shifted(near, "core", 1)

    opp_a = shifted(before[:half], "col", 1)
    opp_b = shifted(after[half:], "col", -1)

    tile = lambda n: pl.BlockSpec((width, n), lambda m: (0, m))
    whole = pl.BlockSpec((width, rows), lambda m: (0, 0))
    step_lanes = PAIRS * LANES
    grams = [(3, width, width), (1, LANES)] * 2
    gram_specs = [pl.BlockSpec((3, width, width), lambda m: (0, 0, 0)), pl.BlockSpec((1, LANES), lambda m: (0, 0))] * 2
    made = call(
        functools.partial(image_kernel, blk * groups),
        [(width, rows)] * 2 + grams + [(modes, rows)] * 4,
        [SMEM] * 2
        + [whole] * 4
        + [pl.BlockSpec((width, rows // 2), lambda m: (0, 0))]
        + [pl.BlockSpec((step_lanes, values.shape[1]), lambda m: (m, 0))]
        + [tile(step_lanes)] * 2
        + [VMEM],
        [jnp.bfloat16] * 2 + [F32] * 8,
        out_specs=[tile(step_lanes)] * 2
        + gram_specs
        + [pl.BlockSpec((modes, step_lanes), lambda m: (0, m))] * 4,
        grid=(rows // step_lanes,),
        scratch_shapes=[pltpu.VMEM((3 * width, LANES), F32)] * 2 + [pltpu.VMEM((4 * modes, width), F32)],
    )(col, cols, st, swap, near, relay, far, values, before, after, ritz)
    image, grams, (part_own, part_after, part_opp, part_before) = made[:2], made[2:6], made[6:]

    payload, terms = call(
        late_kernel,
        [(PARTS, 8 * TILES, LANES), (8, LANES)],
        [SMEM] + [VMEM] * 10,
        scratch_shapes=[pltpu.VMEM((4 * width, width), F32)] * 2,
    )(col, *grams, opp_a, opp_b, *image, st, ritz)

    got = lax.all_to_all(payload, RING, 0, 0, tiled=True)
    around = [shifted(terms, "col", by) for by in (1, 2, 3)]
    from_prev = shifted(part_after, "col", 1)
    from_next = shifted(part_before, "col", -1)
    from_opp = shifted(part_opp, "col", 2)
    new_modes, new_image = call(
        modes_kernel,
        [(modes, rows)] * 2,
        [SMEM] + [VMEM] * 10,
        scratch_shapes=[pltpu.VMEM((4 * modes, width), F32)],
    )(col, st, before, after, opp_a, opp_b, ritz, part_own, from_prev, from_next, from_opp)

    part = jnp.concatenate(
        [jnp.sum(got, axis=0), terms + around[0] + around[1] + around[2]], axis=0
    )
    part = jnp.broadcast_to(part[None], (4,) + part.shape)
    part = lax.all_to_all(part, "zh", 0, 0, tiled=True)
    part = jnp.sum(part, axis=0)
    parts = lax.all_to_all(spread_out(part), RING, 0, 0, tiled=True)

    stiff, mass, theta, residual = call(
        final_kernel,
        [(width, 4 * width), (width, 4 * width), (1, modes), (modes, rows)],
        [SMEM] + [VMEM] * 3,
    )(col, parts, new_modes, new_image)
    return (new_modes.T, residual.T, theta[0], stiff.T, mass.T)


def solution(mesh):
    mesh = Mesh(mesh.devices.reshape(4, 2, 4, 2, 4), WIRE + ("col",))
    return jax.shard_map(
        shards,
        mesh=mesh,
        in_specs=(P(WIRE, "col"), P(WIRE, None), P(WIRE, None), P()),
        out_specs=(P(WIRE, "col"), P(WIRE, "col"), P("col"), P(None, "col"), P(None, "col")),
        check_vma=False,
    )
```

```python
import functools

import jax
import jax.numpy as jnp
from jax import lax
from jax.experimental import pallas as pl
from jax.experimental.pallas import tpu as pltpu
from jax.sharding import Mesh, PartitionSpec as P


RING = ("zl", "y", "core")
WIRE = ("zh", "zl", "y", "core")
BLOCK = 64
PARTS = 16
TILES = 5
PAIRS = 4
LANES = 128
F32 = jnp.float32
NN = (((1,), (0,)), ((), ()))
NT = (((1,), (1,)), ((), ()))
VMEM = pl.BlockSpec(memory_space=pltpu.VMEM)
SMEM = pl.BlockSpec(memory_space=pltpu.SMEM)


def shifted(array, axis, by):
    length = lax.axis_size(axis)
    return lax.ppermute(array, axis, [(i, (i + by) % length) for i in range(length)])


def to_sides(array, distance, back=False):
    length = lax.axis_size(WIRE)
    pairs = [((i - distance if i % 2 == 0 else i + distance) % length, i) for i in range(length)]
    return lax.ppermute(array, WIRE, [pair[::-1] for pair in pairs] if back else pairs)


def split(x):
    high = x.astype(jnp.bfloat16)
    return high, (x - high.astype(F32)).astype(jnp.bfloat16)


def dot3(a, b, dims):
    (ah, al), (bh, bl) = a, b
    one = lambda x, y: lax.dot_general(x, y, dims, preferred_element_type=F32)
    rows = ah.shape[0]
    first = one(jnp.concatenate([ah, al], axis=0), bh)
    return first[:rows] + (first[rows:] + one(ah, bl))


def lane_tile(x):
    short = LANES - x.shape[0]
    return jnp.concatenate([x, jnp.zeros((short, x.shape[1]), x.dtype)], axis=0) if short else x


def dot4(a, b):
    both = lax.dot_general(
        jnp.concatenate(a, axis=0),
        jnp.concatenate([lane_tile(b[0]), lane_tile(b[1])], axis=0),
        NT,
        preferred_element_type=F32,
    )
    rows = a[0].shape[0]
    both = both[:rows] + both[rows:]
    return both[:, :LANES] + both[:, LANES:]


def low_half(shape):
    return lax.broadcasted_iota(jnp.int32, shape, 1) < BLOCK


def tile_at(ref, index):
    return ref[:, pl.ds(pl.multiple_of(index // 2 * LANES, LANES), LANES)]


def in_half(tile, index, half):
    return jnp.where(index % 2 == half, tile, pltpu.roll(tile, BLOCK, 1))


def group_start(here, by, blk, count):
    start = here + by * blk
    return jnp.where(start >= count, start - count, jnp.where(start < 0, start + count, start))


def pack_kernel(cols, asked, st, packed):
    low = low_half((st.shape[0], LANES))
    here = cols[0, 0]
    parity = 1 - here // cols.shape[1] % 2

    def step(m, carry):
        first = asked[3, 4 * m + parity] - here
        second = asked[3, 4 * m + 2 + parity] - here
        packed[:, pl.ds(pl.multiple_of(m * LANES, LANES), LANES)] = jnp.where(
            low, in_half(tile_at(st, first), first, 0), in_half(tile_at(st, second), second, 1)
        )
        return carry

    lax.fori_loop(0, packed.shape[1] // LANES, step, 0, unroll=4)


def coef_kernel(values, high, low):
    for at in range(0, values.shape[0], BLOCK):
        coef = values[at : at + BLOCK, :]
        if at // BLOCK % 2:
            coef = jnp.concatenate([pltpu.roll(coef[:, :LANES], BLOCK, 1), coef[:, LANES:]], axis=1)
        high[at : at + BLOCK, :], low[at : at + BLOCK, :] = split(coef)


def image_kernel(
    count, col, cols, st, swap, near, relay, far, values_high, values_low, before, after, ritz,
    image_high, image_low, stiff, stiff_terms, mass, mass_terms,
    part_own, part_after, part_opp, part_before, stiff_sum, mass_sum, turned
):
    m = pl.program_id(0)
    width = st.shape[0]
    pairs = values_high.shape[0] // LANES
    left_half = low_half((width, LANES))
    images, owns = [], []
    blk = cols.shape[1]
    here = cols[0, 0]
    even = here // blk % 2 == 0
    starts = [group_start(here, by, blk, count) for by in (1, 2, -1, -2)]
    beside = ((swap, near), (near, swap))

    @pl.when(m == 0)
    def _():
        stiff_sum[...] = jnp.zeros_like(stiff_sum)
        mass_sum[...] = jnp.zeros_like(mass_sum)
        turned[...] = ritz[pl.ds(pl.multiple_of(col[0] * width, 8), width), :].T

    modes = part_own.shape[0]
    send = split(
        jnp.concatenate(
            [turned[pl.ds(pl.multiple_of((col[0] + i) % 4 * modes, 8), modes), :] for i in range(4)], axis=0
        )
    )
    for h in range(pairs):
        tile = m * pairs + h
        own = st[:, pl.ds(pl.multiple_of(tile * LANES, LANES), LANES)]
        owns.append(own)
        left = []
        for q in range(2):
            row = 2 * tile + q
            index = cols[1, row] - here
            close = in_half(tile_at(st, index), index, 1 - q)
            first = jnp.where(left_half, own, close) if q == 0 else jnp.where(left_half, close, own)
            index = cols[2, row] - starts[2 * q]
            one, two = (tile_at(ref, index) for ref in beside[q])
            third = in_half(jnp.where(even, one, two), index, 0)
            whole = even if q == 0 else jnp.logical_not(even)
            index = jnp.where(whole, cols[3, row] - starts[2 * q + 1], row // 2)
            last = tile_at(far, row // 2)
            last = jnp.where(whole, tile_at(relay, jnp.where(whole, index, 0)), last)
            beyond = (third, in_half(last, index, 1))
            left.append(jnp.concatenate([first, jnp.where(left_half, *beyond)], axis=1))
        rows = slice(h * LANES, (h + 1) * LANES)
        part = dot4(
            split(jnp.concatenate(left, axis=0)), (values_high[rows, :], values_low[rows, :])
        )
        images.append(split(4.0 * own + jnp.where(left_half, part[:width], part[width:])))
        if h % 2:
            span = slice((h - 1) * LANES, (h + 1) * LANES)
            image = tuple(jnp.concatenate([images[h - 1][i], images[h][i]], axis=1) for i in range(2))
            image_high[:, span], image_low[:, span] = image
            mine = jnp.concatenate(owns[h - 1 :], axis=1)
            pieces = split(jnp.concatenate([mine, before[:, span], after[:, span]], axis=0))
            mass_sum[...] += dot4(pieces, (pieces[0][:width], pieces[1][:width]))
            stiff_sum[...] += dot4(pieces, image)
            part = dot3(send, image, NN)
            for i, out in enumerate((part_own, part_after, part_opp, part_before)):
                out[:, span] = part[i * modes : (i + 1) * modes]

    @pl.when(m == pl.num_programs(0) - 1)
    def _():
        for gram, terms, total in ((stiff, stiff_terms, stiff_sum), (mass, mass_terms, mass_sum)):
            for i in range(3):
                gram[i] = total[i * width : (i + 1) * width, :width]
            piece_terms(gram, col[0], ritz, terms)


def quotient_terms(piece, mine, ritz, start):
    left = dot3(split(piece), split(mine), NN)
    return jnp.sum(left * ritz[pl.ds(start, piece.shape[0]), :], axis=0, keepdims=True)


def piece_terms(gram, c, ritz, terms):
    width = gram.shape[1]
    at = lambda by: pl.multiple_of((c + by) % 4 * width, 8)
    mine = ritz[pl.ds(at(0), width), :]
    total = quotient_terms(gram[0], mine, ritz, at(0))
    total = total + quotient_terms(gram[1], mine, ritz, at(3))
    terms[...] = total + quotient_terms(gram[2], mine, ritz, at(1))


def late_kernel(
    col, stiff3, stiff_terms, mass3, mass_terms, opp_a, opp_b, image_high, image_low, st, ritz,
    payload, terms, stiff, mass
):
    c = col[0]
    width = st.shape[0]
    far = split(jnp.concatenate([opp_a[...], opp_b[...]], axis=0))
    far_stiff = dot4(far, (image_high[...], image_low[...]))[:, :width]
    far_mass = dot4(far, split(st[...]))[:, :width]
    terms[...] = jnp.zeros_like(terms)
    at = lambda by: pl.multiple_of((c + by) % 4 * width, 8)
    mine = ritz[pl.ds(at(0), width), :]
    turned = []
    for i, (block, whole, pieces, sums) in enumerate(
        (
            (far_stiff, stiff, stiff3, stiff_terms),
            (far_mass, mass, mass3, mass_terms),
        )
    ):
        for piece, by in ((pieces[0], 0), (pieces[1], 3), (pieces[2], 1), (block, 2)):
            whole[pl.ds(at(by), width), :] = piece
        terms[i : i + 1, :] = sums[...] + quotient_terms(block, mine, ritz, at(2))
        turned.append(whole[...].T)
    for t in range(PARTS * TILES):
        k, to = t // TILES, t % TILES * 8
        i, j = t // 3 * 8, t % 3 * LANES
        if i < 2 * width:
            payload[k, to : to + 8, :] = turned[i // width][i % width : i % width + 8, j : j + LANES]
        else:
            payload[k, to : to + 8, :] = jnp.zeros((8, LANES), F32)


def modes_kernel(
    col, st, before, after, opp_a, opp_b, ritz, own, from_prev, from_next, from_opp, modes, image, turned
):
    width = st.shape[0]
    coef = []
    for by in (0, 3, 1, 2):
        turned[...] = ritz[pl.ds(pl.multiple_of((col[0] + by) % 4 * width, 8), width), :].T
        coef.append(turned[pl.ds(pl.multiple_of(col[0] * modes.shape[0], 8), modes.shape[0]), :])
    opp = jnp.concatenate([opp_a[...], opp_b[...]], axis=0)
    modes[...] = (
        dot3(split(coef[0]), split(st[...]), NN)
        + dot3(split(coef[1]), split(before[...]), NN)
        + dot3(split(coef[2]), split(after[...]), NN)
        + dot3(split(coef[3]), split(opp), NN)
    )
    image[...] = (own[...] + from_opp[...]) + (from_prev[...] + from_next[...])


def final_kernel(col, parts, modes, image, stiff, mass, theta, residual):
    total = jnp.float32(196608.0)
    terms = parts[0, 8 * TILES :, :]
    for k in range(1, PARTS):
        terms = terms + parts[k, 8 * TILES :, :]
    quotient = terms[0:1, :] / terms[1:2, :]
    shape = (modes.shape[0], LANES)
    here = lax.broadcasted_iota(jnp.int32, shape, 1) == (
        lax.broadcasted_iota(jnp.int32, shape, 0) + col[0] * shape[0]
    )
    column = jnp.sum(jnp.where(here, jnp.broadcast_to(quotient, shape), 0.0), axis=1, keepdims=True)
    theta[...] = pltpu.roll(
        jnp.broadcast_to(quotient, (8, LANES)), (4 - col[0]) % 4 * shape[0], 1
    )[0:1, : shape[0]]
    residual[...] = image[...] - column * modes[...]
    width = stiff.shape[0]
    for t in range(2 * width // 8 * 3):
        k, at = t // TILES, t % TILES * 8
        i, j = t // 3 * 8, t % 3 * LANES
        out = stiff if i < width else mass
        out[i % width : i % width + 8, j : j + LANES] = parts[k, at : at + 8, :] / total


def call(kernel, shapes, in_specs, dtypes=None, **kwargs):
    dtypes = dtypes or [F32] * len(shapes)
    return pl.pallas_call(
        kernel,
        out_shape=[jax.ShapeDtypeStruct(s, d) for s, d in zip(shapes, dtypes)],
        in_specs=in_specs,
        out_specs=kwargs.pop("out_specs", [VMEM] * len(shapes)),
        **kwargs,
    )


def spread_out(part):
    return jnp.broadcast_to(part[None], (PARTS,) + part.shape)


def shards(search, values, block_cols, ritz):
    rows, width = search.shape
    blk = block_cols.shape[0]
    modes = ritz.shape[1] // 4
    half = width // 2
    c = lax.axis_index("col")
    groups = lax.axis_size(WIRE)
    col = jnp.reshape(c, (1,)).astype(jnp.int32)
    st = search.T
    cols = block_cols.T

    before = shifted(st, "col", 1)
    after = shifted(st, "col", -1)
    asked = to_sides(cols, 2, back=True)
    near = to_sides(st, 1)
    swap = shifted(st, "core", 1)
    packed = call(pack_kernel, [(width, rows // 2)], [SMEM] * 2 + [VMEM])(cols, asked, st)[0]
    far = to_sides(packed, 2)
    relay = shifted(near, "core", 1)

    step_lanes = PAIRS * LANES
    depth = values.shape[1]
    coef_spec = pl.BlockSpec((step_lanes, depth), lambda m: (m, 0))
    coefs = call(
        coef_kernel,
        [(rows, depth)] * 2,
        [coef_spec],
        [jnp.bfloat16] * 2,
        out_specs=[coef_spec] * 2,
        grid=(rows // step_lanes,),
    )(values)

    opp_a = shifted(before[:half], "col", 1)
    opp_b = shifted(after[half:], "col", -1)

    tile = lambda n: pl.BlockSpec((width, n), lambda m: (0, m))
    whole = pl.BlockSpec((width, rows), lambda m: (0, 0))
    grams = [(3, width, width), (1, LANES)] * 2
    gram_specs = [pl.BlockSpec((3, width, width), lambda m: (0, 0, 0)), pl.BlockSpec((1, LANES), lambda m: (0, 0))] * 2
    made = call(
        functools.partial(image_kernel, blk * groups),
        [(width, rows)] * 2 + grams + [(modes, rows)] * 4,
        [SMEM] * 2
        + [whole] * 4
        + [pl.BlockSpec((width, rows // 2), lambda m: (0, 0))]
        + [coef_spec] * 2
        + [tile(step_lanes)] * 2
        + [VMEM],
        [jnp.bfloat16] * 2 + [F32] * 8,
        out_specs=[tile(step_lanes)] * 2
        + gram_specs
        + [pl.BlockSpec((modes, step_lanes), lambda m: (0, m))] * 4,
        grid=(rows // step_lanes,),
        scratch_shapes=[pltpu.VMEM((3 * width, LANES), F32)] * 2 + [pltpu.VMEM((4 * modes, width), F32)],
    )(col, cols, st, swap, near, relay, far, *coefs, before, after, ritz)
    image, grams, (part_own, part_after, part_opp, part_before) = made[:2], made[2:6], made[6:]

    payload, terms = call(
        late_kernel,
        [(PARTS, 8 * TILES, LANES), (8, LANES)],
        [SMEM] + [VMEM] * 10,
        scratch_shapes=[pltpu.VMEM((4 * width, width), F32)] * 2,
    )(col, *grams, opp_a, opp_b, *image, st, ritz)

    got = lax.all_to_all(payload, RING, 0, 0, tiled=True)
    around = [shifted(terms, "col", by) for by in (1, 2, 3)]
    from_prev = shifted(part_after, "col", 1)
    from_next = shifted(part_before, "col", -1)
    from_opp = shifted(part_opp, "col", 2)
    new_modes, new_image = call(
        modes_kernel,
        [(modes, rows)] * 2,
        [SMEM] + [VMEM] * 10,
        scratch_shapes=[pltpu.VMEM((4 * modes, width), F32)],
    )(col, st, before, after, opp_a, opp_b, ritz, part_own, from_prev, from_next, from_opp)

    part = jnp.concatenate(
        [jnp.sum(got, axis=0), terms + around[0] + around[1] + around[2]], axis=0
    )
    part = jnp.broadcast_to(part[None], (4,) + part.shape)
    part = lax.all_to_all(part, "zh", 0, 0, tiled=True)
    part = jnp.sum(part, axis=0)
    parts = lax.all_to_all(spread_out(part), RING, 0, 0, tiled=True)

    stiff, mass, theta, residual = call(
        final_kernel,
        [(width, 4 * width), (width, 4 * width), (1, modes), (modes, rows)],
        [SMEM] + [VMEM] * 3,
    )(col, parts, new_modes, new_image)
    return (new_modes.T, residual.T, theta[0], stiff.T, mass.T)


def solution(mesh):
    mesh = Mesh(mesh.devices.reshape(4, 2, 4, 2, 4), WIRE + ("col",))
    return jax.shard_map(
        shards,
        mesh=mesh,
        in_specs=(P(WIRE, "col"), P(WIRE, None), P(WIRE, None), P()),
        out_specs=(P(WIRE, "col"), P(WIRE, "col"), P("col"), P(None, "col"), P(None, "col")),
        check_vma=False,
    )
```

```python
import functools

import jax
import jax.numpy as jnp
from jax import lax
from jax.experimental import pallas as pl
from jax.experimental.pallas import tpu as pltpu
from jax.sharding import Mesh, PartitionSpec as P


RING = ("zl", "y", "core")
WIRE = ("zh", "zl", "y", "core")
BLOCK = 64
PARTS = 16
TILES = 5
PAIRS = 4
LANES = 128
F32 = jnp.float32
NN = (((1,), (0,)), ((), ()))
NT = (((1,), (1,)), ((), ()))
VMEM = pl.BlockSpec(memory_space=pltpu.VMEM)
SMEM = pl.BlockSpec(memory_space=pltpu.SMEM)


def shifted(array, axis, by):
    length = lax.axis_size(axis)
    return lax.ppermute(array, axis, [(i, (i + by) % length) for i in range(length)])


def to_sides(array, distance, back=False):
    length = lax.axis_size(WIRE)
    pairs = [((i - distance if i % 2 == 0 else i + distance) % length, i) for i in range(length)]
    return lax.ppermute(array, WIRE, [pair[::-1] for pair in pairs] if back else pairs)


def split(x):
    high = x.astype(jnp.bfloat16)
    return high, (x - high.astype(F32)).astype(jnp.bfloat16)


def dot3(a, b, dims):
    (ah, al), (bh, bl) = a, b
    one = lambda x, y: lax.dot_general(x, y, dims, preferred_element_type=F32)
    rows = ah.shape[0]
    first = one(jnp.concatenate([ah, al], axis=0), bh)
    return first[:rows] + (first[rows:] + one(ah, bl))


def lane_tile(x):
    short = LANES - x.shape[0]
    return jnp.concatenate([x, jnp.zeros((short, x.shape[1]), x.dtype)], axis=0) if short else x


def dot4(a, b):
    both = lax.dot_general(
        jnp.concatenate(a, axis=0),
        jnp.concatenate([lane_tile(b[0]), lane_tile(b[1])], axis=0),
        NT,
        preferred_element_type=F32,
    )
    rows = a[0].shape[0]
    both = both[:rows] + both[rows:]
    return both[:, :LANES] + both[:, LANES:]


def low_half(shape):
    return lax.broadcasted_iota(jnp.int32, shape, 1) < BLOCK


def tile_at(ref, index):
    return ref[:, pl.ds(pl.multiple_of(index // 2 * LANES, LANES), LANES)]


def in_half(tile, index, half):
    return jnp.where(index % 2 == half, tile, pltpu.roll(tile, BLOCK, 1))


def group_start(here, by, blk, count):
    start = here + by * blk
    return jnp.where(start >= count, start - count, jnp.where(start < 0, start + count, start))


def pack_kernel(cols, asked, st, packed):
    low = low_half((st.shape[0], LANES))
    here = cols[0, 0]
    parity = 1 - here // cols.shape[1] % 2

    def step(m, carry):
        first = asked[3, 4 * m + parity] - here
        second = asked[3, 4 * m + 2 + parity] - here
        packed[:, pl.ds(pl.multiple_of(m * LANES, LANES), LANES)] = jnp.where(
            low, in_half(tile_at(st, first), first, 0), in_half(tile_at(st, second), second, 1)
        )
        return carry

    lax.fori_loop(0, packed.shape[1] // LANES, step, 0, unroll=4)


def coef_kernel(values, high, low):
    for at in range(0, values.shape[0], BLOCK):
        coef = values[at : at + BLOCK, :]
        if at // BLOCK % 2:
            coef = jnp.concatenate([pltpu.roll(coef[:, :LANES], BLOCK, 1), coef[:, LANES:]], axis=1)
        high[at : at + BLOCK, :], low[at : at + BLOCK, :] = split(coef)


def image_kernel(
    count, col, cols, st, swap, near, relay, far, values_high, values_low, before, after, ritz,
    image_high, image_low, stiff, stiff_terms, mass, mass_terms,
    part_own, part_after, part_opp, part_before, stiff_sum, mass_sum, turned
):
    m = pl.program_id(0)
    width = st.shape[0]
    pairs = values_high.shape[0] // LANES
    left_half = low_half((width, LANES))
    images, owns = [], []
    blk = cols.shape[1]
    here = cols[0, 0]
    even = here // blk % 2 == 0
    starts = [group_start(here, by, blk, count) for by in (1, 2, -1, -2)]
    beside = ((swap, near), (near, swap))

    @pl.when(m == 0)
    def _():
        stiff_sum[...] = jnp.zeros_like(stiff_sum)
        mass_sum[...] = jnp.zeros_like(mass_sum)
        turned[...] = ritz[pl.ds(pl.multiple_of(col[0] * width, 8), width), :].T

    modes = part_own.shape[0]
    send = split(
        jnp.concatenate(
            [turned[pl.ds(pl.multiple_of((col[0] + i) % 4 * modes, 8), modes), :] for i in range(4)], axis=0
        )
    )
    for h in range(pairs):
        tile = m * pairs + h
        own = st[:, pl.ds(pl.multiple_of(tile * LANES, LANES), LANES)]
        owns.append(own)
        left = []
        for q in range(2):
            row = 2 * tile + q
            index = cols[1, row] - here
            close = in_half(tile_at(st, index), index, 1 - q)
            first = jnp.where(left_half, own, close) if q == 0 else jnp.where(left_half, close, own)
            index = cols[2, row] - starts[2 * q]
            one, two = (tile_at(ref, index) for ref in beside[q])
            third = in_half(jnp.where(even, one, two), index, 0)
            whole = even if q == 0 else jnp.logical_not(even)
            index = jnp.where(whole, cols[3, row] - starts[2 * q + 1], row // 2)
            last = tile_at(far, row // 2)
            last = jnp.where(whole, tile_at(relay, jnp.where(whole, index, 0)), last)
            beyond = (third, in_half(last, index, 1))
            left.append(jnp.concatenate([first, jnp.where(left_half, *beyond)], axis=1))
        rows = slice(h * LANES, (h + 1) * LANES)
        part = dot4(
            split(jnp.concatenate(left, axis=0)), (values_high[rows, :], values_low[rows, :])
        )
        images.append(split(4.0 * own + jnp.where(left_half, part[:width], part[width:])))
        if h % 2:
            span = slice((h - 1) * LANES, (h + 1) * LANES)
            image = tuple(jnp.concatenate([images[h - 1][i], images[h][i]], axis=1) for i in range(2))
            image_high[:, span], image_low[:, span] = image
            mine = jnp.concatenate(owns[h - 1 :], axis=1)
            pieces = split(jnp.concatenate([mine, before[:, span], after[:, span]], axis=0))
            mass_sum[...] += dot4(pieces, (pieces[0][:width], pieces[1][:width]))
            stiff_sum[...] += dot4(pieces, image)
            part = dot3(send, image, NN)
            for i, out in enumerate((part_own, part_after, part_opp, part_before)):
                out[:, span] = part[i * modes : (i + 1) * modes]

    @pl.when(m == pl.num_programs(0) - 1)
    def _():
        for gram, terms, total in ((stiff, stiff_terms, stiff_sum), (mass, mass_terms, mass_sum)):
            for i in range(3):
                gram[i] = total[i * width : (i + 1) * width, :width]
            piece_terms(gram, col[0], ritz, terms)


def quotient_terms(piece, mine, ritz, start):
    left = dot3(split(piece), split(mine), NN)
    return jnp.sum(left * ritz[pl.ds(start, piece.shape[0]), :], axis=0, keepdims=True)


def piece_terms(gram, c, ritz, terms):
    width = gram.shape[1]
    at = lambda by: pl.multiple_of((c + by) % 4 * width, 8)
    mine = ritz[pl.ds(at(0), width), :]
    total = quotient_terms(gram[0], mine, ritz, at(0))
    total = total + quotient_terms(gram[1], mine, ritz, at(3))
    terms[...] = total + quotient_terms(gram[2], mine, ritz, at(1))


def late_kernel(
    col, stiff3, stiff_terms, mass3, mass_terms, opp_a, opp_b, image_high, image_low, st, ritz,
    payload, terms, stiff, mass
):
    c = col[0]
    width = st.shape[0]
    far = split(jnp.concatenate([opp_a[...], opp_b[...]], axis=0))
    far_stiff = dot4(far, (image_high[...], image_low[...]))[:, :width]
    far_mass = dot4(far, split(st[...]))[:, :width]
    terms[...] = jnp.zeros_like(terms)
    at = lambda by: pl.multiple_of((c + by) % 4 * width, 8)
    mine = ritz[pl.ds(at(0), width), :]
    turned = []
    for i, (block, whole, pieces, sums) in enumerate(
        (
            (far_stiff, stiff, stiff3, stiff_terms),
            (far_mass, mass, mass3, mass_terms),
        )
    ):
        for piece, by in ((pieces[0], 0), (pieces[1], 3), (pieces[2], 1), (block, 2)):
            whole[pl.ds(at(by), width), :] = piece
        terms[i : i + 1, :] = sums[...] + quotient_terms(block, mine, ritz, at(2))
        turned.append(whole[...].T)
    for t in range(PARTS * TILES):
        k, to = t // TILES, t % TILES * 8
        i, j = t // 3 * 8, t % 3 * LANES
        if i < 2 * width:
            payload[k, to : to + 8, :] = turned[i // width][i % width : i % width + 8, j : j + LANES]
        else:
            payload[k, to : to + 8, :] = jnp.zeros((8, LANES), F32)


def join_kernel(got, own, next_one, next_two, next_three, out):
    total = got[0]
    for k in range(1, got.shape[0]):
        total = total + got[k]
    terms = own[...] + next_one[...] + next_two[...] + next_three[...]
    for k in range(out.shape[0]):
        out[k, : total.shape[0], :] = total
        out[k, total.shape[0] :, :] = terms


def modes_kernel(
    col, st, before, after, opp_a, opp_b, ritz, own, from_prev, from_next, from_opp, modes, image, turned
):
    width = st.shape[0]
    coef = []
    for by in (0, 3, 1, 2):
        turned[...] = ritz[pl.ds(pl.multiple_of((col[0] + by) % 4 * width, 8), width), :].T
        coef.append(turned[pl.ds(pl.multiple_of(col[0] * modes.shape[0], 8), modes.shape[0]), :])
    opp = jnp.concatenate([opp_a[...], opp_b[...]], axis=0)
    modes[...] = (
        dot3(split(coef[0]), split(st[...]), NN)
        + dot3(split(coef[1]), split(before[...]), NN)
        + dot3(split(coef[2]), split(after[...]), NN)
        + dot3(split(coef[3]), split(opp), NN)
    )
    image[...] = (own[...] + from_opp[...]) + (from_prev[...] + from_next[...])


def final_kernel(col, parts, modes, image, stiff, mass, theta, residual):
    total = jnp.float32(196608.0)
    terms = parts[0, 8 * TILES :, :]
    for k in range(1, PARTS):
        terms = terms + parts[k, 8 * TILES :, :]
    quotient = terms[0:1, :] / terms[1:2, :]
    shape = (modes.shape[0], LANES)
    here = lax.broadcasted_iota(jnp.int32, shape, 1) == (
        lax.broadcasted_iota(jnp.int32, shape, 0) + col[0] * shape[0]
    )
    column = jnp.sum(jnp.where(here, jnp.broadcast_to(quotient, shape), 0.0), axis=1, keepdims=True)
    theta[...] = pltpu.roll(
        jnp.broadcast_to(quotient, (8, LANES)), (4 - col[0]) % 4 * shape[0], 1
    )[0:1, : shape[0]]
    residual[...] = image[...] - column * modes[...]
    width = stiff.shape[0]
    for t in range(2 * width // 8 * 3):
        k, at = t // TILES, t % TILES * 8
        i, j = t // 3 * 8, t % 3 * LANES
        out = stiff if i < width else mass
        out[i % width : i % width + 8, j : j + LANES] = parts[k, at : at + 8, :] / total


def call(kernel, shapes, in_specs, dtypes=None, **kwargs):
    dtypes = dtypes or [F32] * len(shapes)
    return pl.pallas_call(
        kernel,
        out_shape=[jax.ShapeDtypeStruct(s, d) for s, d in zip(shapes, dtypes)],
        in_specs=in_specs,
        out_specs=kwargs.pop("out_specs", [VMEM] * len(shapes)),
        **kwargs,
    )


def spread_out(part):
    return jnp.broadcast_to(part[None], (PARTS,) + part.shape)


def shards(search, values, block_cols, ritz):
    rows, width = search.shape
    blk = block_cols.shape[0]
    modes = ritz.shape[1] // 4
    half = width // 2
    c = lax.axis_index("col")
    groups = lax.axis_size(WIRE)
    col = jnp.reshape(c, (1,)).astype(jnp.int32)
    st = search.T
    cols = block_cols.T

    before = shifted(st, "col", 1)
    after = shifted(st, "col", -1)
    asked = to_sides(cols, 2, back=True)
    near = to_sides(st, 1)
    swap = shifted(st, "core", 1)
    packed = call(pack_kernel, [(width, rows // 2)], [SMEM] * 2 + [VMEM])(cols, asked, st)[0]
    far = to_sides(packed, 2)
    relay = shifted(near, "core", 1)

    step_lanes = PAIRS * LANES
    depth = values.shape[1]
    coef_spec = pl.BlockSpec((step_lanes, depth), lambda m: (m, 0))
    coefs = call(
        coef_kernel,
        [(rows, depth)] * 2,
        [coef_spec],
        [jnp.bfloat16] * 2,
        out_specs=[coef_spec] * 2,
        grid=(rows // step_lanes,),
    )(values)

    opp_a = shifted(before[:half], "col", 1)
    opp_b = shifted(after[half:], "col", -1)

    tile = lambda n: pl.BlockSpec((width, n), lambda m: (0, m))
    whole = pl.BlockSpec((width, rows), lambda m: (0, 0))
    grams = [(3, width, width), (1, LANES)] * 2
    gram_specs = [pl.BlockSpec((3, width, width), lambda m: (0, 0, 0)), pl.BlockSpec((1, LANES), lambda m: (0, 0))] * 2
    made = call(
        functools.partial(image_kernel, blk * groups),
        [(width, rows)] * 2 + grams + [(modes, rows)] * 4,
        [SMEM] * 2
        + [whole] * 4
        + [pl.BlockSpec((width, rows // 2), lambda m: (0, 0))]
        + [coef_spec] * 2
        + [tile(step_lanes)] * 2
        + [VMEM],
        [jnp.bfloat16] * 2 + [F32] * 8,
        out_specs=[tile(step_lanes)] * 2
        + gram_specs
        + [pl.BlockSpec((modes, step_lanes), lambda m: (0, m))] * 4,
        grid=(rows // step_lanes,),
        scratch_shapes=[pltpu.VMEM((3 * width, LANES), F32)] * 2 + [pltpu.VMEM((4 * modes, width), F32)],
    )(col, cols, st, swap, near, relay, far, *coefs, before, after, ritz)
    image, grams, (part_own, part_after, part_opp, part_before) = made[:2], made[2:6], made[6:]

    payload, terms = call(
        late_kernel,
        [(PARTS, 8 * TILES, LANES), (8, LANES)],
        [SMEM] + [VMEM] * 10,
        scratch_shapes=[pltpu.VMEM((4 * width, width), F32)] * 2,
    )(col, *grams, opp_a, opp_b, *image, st, ritz)

    got = lax.all_to_all(payload, RING, 0, 0, tiled=True)
    around = [shifted(terms, "col", by) for by in (1, 2, 3)]
    from_prev = shifted(part_after, "col", 1)
    from_next = shifted(part_before, "col", -1)
    from_opp = shifted(part_opp, "col", 2)
    new_modes, new_image = call(
        modes_kernel,
        [(modes, rows)] * 2,
        [SMEM] + [VMEM] * 10,
        scratch_shapes=[pltpu.VMEM((4 * modes, width), F32)],
    )(col, st, before, after, opp_a, opp_b, ritz, part_own, from_prev, from_next, from_opp)

    part = call(join_kernel, [(4, 8 * TILES + 8, LANES)], [VMEM] * 5)(got, terms, *around)[0]
    part = lax.all_to_all(part, "zh", 0, 0, tiled=True)
    part = jnp.sum(part, axis=0)
    parts = lax.all_to_all(spread_out(part), RING, 0, 0, tiled=True)

    stiff, mass, theta, residual = call(
        final_kernel,
        [(width, 4 * width), (width, 4 * width), (1, modes), (modes, rows)],
        [SMEM] + [VMEM] * 3,
    )(col, parts, new_modes, new_image)
    return (new_modes.T, residual.T, theta[0], stiff.T, mass.T)


def solution(mesh):
    mesh = Mesh(mesh.devices.reshape(4, 2, 4, 2, 4), WIRE + ("col",))
    return jax.shard_map(
        shards,
        mesh=mesh,
        in_specs=(P(WIRE, "col"), P(WIRE, None), P(WIRE, None), P()),
        out_specs=(P(WIRE, "col"), P(WIRE, "col"), P("col"), P(None, "col"), P(None, "col")),
        check_vma=False,
    )
```
